32 devices in a mesh: tx: 8 (over y, x, core), ty: 4 (over z).
Axes of the slice: x: 2, y: 2, z: 4, core: 2. Of those that a mesh axis runs over, the one named last changes fastest.
Arguments:
- offsets: float32 [2, 16, 16, 128], P(None, 'tx', 'ty'), may hold values from 0 to 1
- circ: float32 [16, 16, 128], P('tx', 'ty'), as said below
- counts: int32 [16, 16], P('tx', 'ty'), may hold values from 1 to 128, as said below
Outputs:
- velocity: float32 [2, 16, 16, 128], P(None, 'tx', 'ty')
- moved: float32 [2, 16, 16, 128], P(None, 'tx', 'ty')
The draws below stay inside these ranges and needn't reach their ends.
Inputs may be any that keep to these rules, and one draw needn't show every extreme that they name: counts of live slots in each cell; at least one cell holds 128; the middle quarter of the cell rows holds more on average. `circ`: circulations of order 0.02 / sqrt(128), of both signs.
All inputs are finite; a program needn't handle non-finite values.
Results may differ from the reference program's by a relative error of at most 0.00011.
Values sent between devices are 32-bit elements; how exact they have to be, the bound alone decides.
No kernel may reach another device: no remote copies, remote signals or barrier semaphores. Data moves between devices by JAX's collectives and lax.ppermute only.
A program may use at most 64 MiB of HBM per device.

```python
import math
import jax
import jax.numpy as jnp
from jax import lax

MODES = 64
P_SIZE = 128
NCELL = 16


def draw_counts(key, part):
    first_key, second = jax.random.split(jax.random.fold_in(key, 11))
    base_count = jax.random.randint(first_key, (NCELL, NCELL), 1, P_SIZE + 1)
    extra_count = jax.random.randint(second, (NCELL, NCELL), 1, P_SIZE + 1)
    row_index = jnp.arange(NCELL, dtype=jnp.int32)[:, None]
    in_band = (row_index >= 3 * NCELL // 8) & (row_index < 5 * NCELL // 8)
    counts = jnp.where(in_band, jnp.maximum(base_count, extra_count), base_count)
    return counts.at[0, 0].set(P_SIZE).astype(jnp.int32)


def draw_circ(key, part):
    first_key, second = jax.random.split(jax.random.fold_in(key, 23))
    rough_part = jnp.clip(jax.random.normal(first_key, (NCELL, NCELL, P_SIZE), jnp.float32), -5.0, 5.0)
    spread = jnp.exp(jax.random.uniform(second, (NCELL, NCELL, P_SIZE), jnp.float32, -1.15, 1.15))
    scale_factor = 0.014 / math.sqrt(P_SIZE)
    return scale_factor * rough_part * spread


def shard_levels(own_key, shape, pieces, least, high):
    factor_of = 1.0
    for axis_at, parts in pieces:
        heights = jax.random.uniform(jax.random.fold_in(jax.random.fold_in(own_key, 6), axis_at), (parts,), jnp.float32, least / len(pieces), high / len(pieces))
        factor_of = factor_of * jnp.repeat(jnp.exp(heights), shape[axis_at] // parts).reshape((-1,) + (1,) * (len(shape) - 1 - axis_at))
    return factor_of


def setup_inputs(seed: int = 0) -> dict:
    key_list = jax.random.split(jax.random.key(seed), 4)
    offsets = jnp.clip(1.0 * jax.random.uniform(key_list[0], (2, NCELL, NCELL, P_SIZE), jnp.float32) ** shard_levels(key_list[0], (2, NCELL, NCELL, P_SIZE), ((1, 8), (2, 4)), -0.2, 0.2), 0.0, 1.0)
    circ = draw_circ(jax.random.fold_in(key_list[3], 71), 0)
    counts = draw_counts(jax.random.fold_in(key_list[3], 71), 0)
    return dict(offsets=offsets, circ=circ, counts=counts)


two_pi = 2.0 * math.pi
screen = 1.5625
smooth = 0.0625
section_step = 0.25


def pair_sum(target, source, shift_rows, shift_cols):
    offset_x = target[0][:, :, None] - source[0][:, None, :] - shift_cols
    offset_y = target[1][:, :, None] - source[1][:, None, :] - shift_rows
    square = offset_x * offset_x + offset_y * offset_y
    weight = source[2][:, None, :] * jnp.exp(-screen * square) / (square + smooth)
    return jnp.stack([jnp.sum(-offset_y * weight, axis=2), jnp.sum(offset_x * weight, axis=2)])


def near_row(window):
    span_cols = window.shape[2] - 2
    target = window[:, 1, 1:1 + span_cols]
    summed = jnp.zeros((2,) + target.shape[1:], jnp.float32)
    for shift_rows in (-1, 0, 1):
        for shift_cols in (-1, 0, 1):
            source = window[:, 1 + shift_rows, 1 + shift_cols:1 + shift_cols + span_cols]
            summed = summed + pair_sum(target, source, float(shift_rows), float(shift_cols))
    return summed


def wave_numbers():
    return (jnp.arange(MODES, dtype=jnp.int32) - MODES // 2).astype(jnp.float32)


def mode_grid(cell_count):
    wave_number = wave_numbers()
    wave_x = two_pi * wave_number[:, None] * jnp.ones((1, MODES), jnp.float32)
    wave_y = two_pi * wave_number[None, :] * jnp.ones((MODES, 1), jnp.float32)
    square = wave_x * wave_x + wave_y * wave_y
    edge_mode = wave_number == -(MODES // 2)
    zero_mode = wave_number == 0
    keep_mode = jnp.logical_not(edge_mode[:, None] | edge_mode[None, :] | (zero_mode[:, None] & zero_mode[None, :]))
    safe_square = jnp.where(keep_mode, square, 1.0)
    damping = jnp.where(keep_mode, jnp.exp(-safe_square / (6.25 * cell_count * cell_count)) / safe_square, 0.0)
    return damping, wave_x, wave_y


def tables(coord):
    phase_angle = two_pi * wave_numbers()[:, None] * coord[None, :]
    return jnp.cos(phase_angle), jnp.sin(phase_angle)


def contract(left_side, right_side):
    return lax.dot_general(left_side, right_side, (((1,), (1,)), ((), ())), precision=lax.Precision.HIGHEST, preferred_element_type=jnp.float32)


def product(left_side, right_side):
    return jnp.dot(left_side, right_side, precision=lax.Precision.HIGHEST, preferred_element_type=jnp.float32)


def structure(x_position, y_position, strength):
    cos_x, sin_x = tables(x_position)
    cos_y, sin_y = tables(y_position)
    real_part = contract(strength * cos_x, cos_y) - contract(strength * sin_x, sin_y)
    imag_part = contract(strength * sin_x, cos_y) + contract(strength * cos_x, sin_y)
    return jnp.stack([real_part, imag_part])


def far_velocity(x_position, y_position, scaled, wave_x, wave_y):
    cos_x, sin_x = tables(x_position)
    cos_y, sin_y = tables(y_position)
    with_imag = jnp.concatenate([wave_y * scaled[1], -wave_x * scaled[1]])
    with_real = jnp.concatenate([wave_y * scaled[0], -wave_x * scaled[0]])
    term_cos = (product(with_imag, cos_y) - product(with_real, sin_y)).reshape(2, MODES, -1)
    term_sin = (product(with_real, cos_y) + product(with_imag, sin_y)).reshape(2, MODES, -1)
    return jnp.sum(cos_x[None] * term_cos - sin_x[None] * term_sin, axis=1)


def reference(offsets, circ, counts):
    live_slot = jnp.arange(P_SIZE, dtype=jnp.int32)[None, None, :] < counts[:, :, None]
    strength = jnp.where(live_slot, circ, 0.0)
    packed = jnp.stack([offsets[0], offsets[1], strength])
    padded = jnp.pad(packed, ((0, 0), (1, 1), (1, 1), (0, 0)), mode="wrap")
    near_part = lax.map(lambda first_row: near_row(lax.dynamic_slice_in_dim(padded, first_row, 3, 1)), jnp.arange(NCELL, dtype=jnp.int32))
    near_part = jnp.transpose(near_part, (1, 0, 2, 3)) * (NCELL / two_pi)
    cell_pos = jnp.arange(NCELL, dtype=jnp.int32).astype(jnp.float32)
    x_position = (cell_pos[None, :, None] + offsets[0]) / NCELL
    y_position = (cell_pos[:, None, None] + offsets[1]) / NCELL

    def row_modes(row_index):
        return structure(x_position[row_index].reshape(-1), y_position[row_index].reshape(-1), strength[row_index].reshape(-1))

    partial_modes = lax.map(row_modes, jnp.arange(NCELL, dtype=jnp.int32))
    summed = jnp.sum(partial_modes, axis=0)
    damping, wave_x, wave_y = mode_grid(NCELL)
    scaled = damping[None] * summed

    def row_far(row_index):
        return far_velocity(x_position[row_index].reshape(-1), y_position[row_index].reshape(-1), scaled, wave_x, wave_y).reshape(2, NCELL, P_SIZE)

    far_part = lax.map(row_far, jnp.arange(NCELL, dtype=jnp.int32))
    far_part = jnp.transpose(far_part, (1, 0, 2, 3))
    velocity = jnp.where(live_slot[None], near_part + far_part, 0.0)
    moved = offsets + section_step * velocity
    return velocity, moved
```

```python
import functools
import math

import jax
import jax.numpy as jnp
from jax import lax
from jax.experimental import pallas as pl
from jax.experimental.pallas import tpu as pltpu
from jax.sharding import PartitionSpec as P


MODES = 64
HALF = MODES // 2

two_pi = 2.0 * math.pi
screen = 1.5625
smooth = 0.0625
section_step = 0.25
unit = math.sqrt(screen / math.log(2.0))
floor_term = smooth * unit * unit

VMEM = pl.BlockSpec(memory_space=pltpu.VMEM)
SMEM = pl.BlockSpec(memory_space=pltpu.SMEM)
PARAMS = pltpu.CompilerParams(vmem_limit_bytes=8 * 1024 * 1024)


def call(body, out_shapes, scratch, flops, *args):
    specs = [SMEM if a.dtype == jnp.int32 else VMEM for a in args]
    outs = [jax.ShapeDtypeStruct(s, d) for s, d in out_shapes]
    return pl.pallas_call(
        body,
        out_shape=outs,
        in_specs=specs,
        out_specs=[VMEM] * len(outs),
        scratch_shapes=scratch,
        compiler_params=PARAMS,
        cost_estimate=pl.CostEstimate(flops=flops, bytes_accessed=65536, transcendentals=0),
    )(*args)


def cell_rows(ref, rows):
    return jnp.concatenate([ref[r] for r in range(rows)], axis=0)


def count_grid(counts_ref, rows, cols, shape):
    cell = lax.broadcasted_iota(jnp.int32, shape, 0)
    limit = jnp.zeros(shape, jnp.int32)
    for r in range(rows):
        for c in range(cols):
            limit = jnp.where(cell == r * cols + c, counts_ref[r, c], limit)
    return lax.broadcasted_iota(jnp.int32, shape, 1) < limit


def unit_circle(turn):
    quarter = jnp.floor(4.0 * turn + 0.5)
    angle = two_pi * (turn - 0.25 * quarter)
    sq = angle * angle
    sine = angle * (
        1.0 + sq * (-1.0 / 6 + sq * (1.0 / 120 + sq * (-1.0 / 5040 + sq * (1.0 / 362880))))
    )
    cosine = 1.0 + sq * (
        -0.5 + sq * (1.0 / 24 + sq * (-1.0 / 720 + sq * (1.0 / 40320 + sq * (-1.0 / 3628800))))
    )
    odd = (quarter == 1.0) | (quarter == 3.0)
    cos_neg = (quarter == 1.0) | (quarter == 2.0)
    sin_neg = (quarter == 2.0) | (quarter == 3.0)
    cos_part = jnp.where(odd, sine, cosine)
    sin_part = jnp.where(odd, cosine, sine)
    return jnp.where(cos_neg, -cos_part, cos_part), jnp.where(sin_neg, -sin_part, sin_part)


def times(p, q):
    return p[0] * q[0] - p[1] * q[1], p[0] * q[1] + p[1] * q[0]


def split(value):
    high = value.astype(jnp.bfloat16)
    low = (value - high.astype(jnp.float32)).astype(jnp.bfloat16)
    return high, low


def moments_kernel(
    rows, cols, cell_count, place, offsets, counts, circ, own, x_table, y_table, powers, weighted
):
    cells = rows * cols
    slots = circ.shape[2]
    shape = (cells, slots)
    cell = lax.broadcasted_iota(jnp.int32, shape, 0)
    row_in = jnp.zeros(shape, jnp.int32)
    for r in range(1, rows):
        row_in = jnp.where(cell >= r * cols, r, row_in)
    col_in = cell - row_in * cols
    live = count_grid(counts, rows, cols, shape)
    strength = jnp.where(live, cell_rows(circ, rows), 0.0)
    off_x = cell_rows(offsets.at[0], rows)
    off_y = cell_rows(offsets.at[1], rows)
    x_turn = ((place[1] * cols + col_in).astype(jnp.float32) + off_x) / cell_count
    y_turn = ((place[0] * rows + row_in).astype(jnp.float32) + off_y) / cell_count
    own[4] = unit * (col_in.astype(jnp.float32) + off_x)
    own[5] = unit * ((place[2] * rows + row_in).astype(jnp.float32) + off_y)
    own[6] = strength * (unit * cell_count / two_pi)
    for axis, turn in ((0, x_turn), (1, y_turn)):
        point = unit_circle(turn)
        for power in range(5):
            powers[axis, power, 0] = point[0]
            powers[axis, power, 1] = point[1]
            if power < 4:
                point = times(point, point)
    powers[0, 0, 2] = strength
    mode = lax.broadcasted_iota(jnp.int32, (8, slots), 0)
    bits = [(mode & (1 << b)) != 0 for b in range(3)]
    for i in range(cells):
        lanes = pl.ds(i * slots, slots)
        amount = jnp.broadcast_to(powers[0, 0, 2, pl.ds(i, 1), :], (8, slots))
        for axis in range(2):

            def row(power, part):
                return jnp.broadcast_to(powers[axis, power, part, pl.ds(i, 1), :], (8, slots))

            group = None
            for b in range(3):
                factor = (jnp.where(bits[b], row(b, 0), 1.0), jnp.where(bits[b], row(b, 1), 0.0))
                group = factor if group is None else times(group, factor)
            eight = (row(3, 0), row(3, 1))
            sixteen = (row(4, 0), row(4, 1))
            second = times(group, eight)
            groups = [group, second, times(group, sixteen), times(second, sixteen)]
            wave = jnp.concatenate([g[0] for g in groups] + [g[1] for g in groups], axis=0)
            if axis == 0:
                x_table[:, lanes] = wave
                high, low = split(wave * jnp.concatenate([amount] * 8, axis=0))
                weighted[0:MODES, lanes] = high
                weighted[MODES : 2 * MODES, lanes] = low
            else:
                high, low = split(wave)
                y_table[0:MODES, lanes] = high
                y_table[MODES : 2 * MODES, lanes] = low
    full = lax.dot_general(
        weighted[...],
        y_table[...],
        (((1,), (1,)), ((), ())),
        preferred_element_type=jnp.float32,
    )
    full = full[0:MODES] + full[MODES : 2 * MODES]
    full = full + pltpu.roll(full, MODES, 1)
    lane = lax.broadcasted_iota(jnp.int32, (HALF, 2 * MODES), 1)
    own[0:4] = jnp.where(lane < MODES, full[0:HALF], full[HALF:MODES]).reshape(4, 8, 2 * MODES)


def pair_terms(target, source, total):
    offset_x = target[0] - source[0]
    offset_y = target[1] - source[1]
    square = offset_x * offset_x + offset_y * offset_y
    weight = source[2] / ((square + floor_term) * jnp.exp2(square))
    return total[0] - offset_y * weight, total[1] + offset_x * weight


def near_sum(sources, targets, links, turned):
    slots = sources[0][0].shape[1]
    stack = [part for source in sources for part in source]
    pad = -len(stack) % 8
    stack = jnp.concatenate(stack + [jnp.zeros((pad, slots), jnp.float32)] * (pad > 0), axis=0)
    turned[:, 0 : stack.shape[0]] = stack.T
    spread = [tuple(jnp.broadcast_to(part, (8, slots)) for part in t) for t in targets]

    def step(k, totals):
        totals = list(totals)
        chunk = turned[pl.ds(pl.multiple_of(8 * k, 8), 8), :]
        for i, reached in enumerate(links):
            source = tuple(
                jnp.broadcast_to(chunk[:, 3 * i + part : 3 * i + part + 1], (8, slots))
                for part in range(3)
            )
            for t in reached:
                totals[2 * t], totals[2 * t + 1] = pair_terms(
                    spread[t], source, (totals[2 * t], totals[2 * t + 1])
                )
        return tuple(totals)

    zero = jnp.zeros((8, slots), jnp.float32)
    totals = (zero,) * (2 * len(targets))
    totals = lax.fori_loop(
        0, slots // 16, lambda k, held: step(2 * k + 1, step(2 * k, held)), totals
    )
    return [jnp.sum(total, axis=0, keepdims=True) for total in totals]


def reach(col, cols):
    return [c for c in (col - 1, col, col + 1) if 0 <= c < cols]


def read_row(ref, base, at):
    return tuple(ref[base + part, pl.ds(at, 1), :] for part in range(3))


def near_local(rows, cols, own, cells, near, turned):
    places = sorted({(r, c) for row, col in cells for r in range(rows) if abs(r - row) <= 1 for c in reach(col, cols)})
    sources = [read_row(own, 4, r * cols + c) for r, c in cells]
    targets = [read_row(own, 4, r * cols + c)[:2] for r, c in places]
    links = [
        [t for t, (r, c) in enumerate(places) if abs(r - row) <= 1 and abs(c - col) <= 1]
        for row, col in cells
    ]
    sums = near_sum(sources, targets, links, turned)
    for t, (r, c) in enumerate(places):
        for part in range(2):
            at = pl.ds(r * cols + c, 1)
            near[part, at, :] = near[part, at, :] + sums[2 * t + part]


def near_local_kernel(rows, cols, cells, own, near, turned):
    near[...] = jnp.zeros_like(near)
    near_local(rows, cols, own, cells, near, turned)


def near_rows(rows, cols, own, outer, base, above, near, turned):
    def pick(ref, origin, part, first, second):
        return jnp.where(
            above == 1, ref[origin + part, pl.ds(first, 1), :], ref[origin + part, pl.ds(second, 1), :]
        )

    sources = [
        tuple(pick(outer, base, part, cols + c, c) for part in range(3)) for c in range(cols)
    ]
    last = (rows - 1) * cols
    targets = [tuple(pick(own, 4, part, c, last + c) for part in range(2)) for c in range(cols)]
    sums = near_sum(sources, targets, [reach(c, cols) for c in range(cols)], turned)
    top = jnp.where(above == 1, 0, last)
    for c in range(cols):
        for part in range(2):
            at = pl.ds(top + c, 1)
            near[part, at, :] = near[part, at, :] + sums[2 * c + part]


def near_cols(rows, cols, own, side, base, core, right, near, turned):
    shift = jnp.where(right == 1, unit * cols, -unit * cols)
    sources = []
    for k in range(rows + 2):
        row = read_row(side, base, core * rows + k)
        sources.append((row[0] + shift, row[1], row[2]))
    edge = jnp.where(right == 1, cols - 1, 0)
    targets = [read_row(own, 4, r * cols + edge)[:2] for r in range(rows)]
    links = [[r for r in range(rows) if 0 <= k - r <= 2] for k in range(rows + 2)]
    sums = near_sum(sources, targets, links, turned)
    for r in range(rows):
        for part in range(2):
            at = pl.ds(r * cols + edge, 1)
            near[part, at, :] = near[part, at, :] + sums[2 * r + part]


def near_partner_kernel(rows, cols, cells, place, own, partner, near, turned):
    near[...] = jnp.zeros_like(near)
    near_local(rows, cols, own, cells, near, turned)
    near_rows(rows, cols, own, partner, 4, place[2], near, turned)


def near_ring_kernel(rows, cols, place, own, packed, near, turned):
    near[...] = jnp.zeros_like(near)
    near_rows(rows, cols, own, packed, 10, 1 - place[2], near, turned)


def near_close_kernel(rows, cols, place, own, close, near, turned):
    near[...] = jnp.zeros_like(near)
    right = 1 - lax.rem(place[1], 2)
    near_cols(rows, cols, own, close, 0, place[2], right, near, turned)


def pack_kernel(rows, cols, place, own, partner, ring, packed):
    core = place[2]
    packed[4:10] = jnp.zeros((6,) + packed.shape[1:], jnp.float32)
    packed[0:4] = ring[0:4]
    for edge, col in ((0, 0), (1, cols - 1)):
        for part in range(3):
            at = 4 + 3 * edge + part
            packed[at, pl.ds(0, 1), :] = ring[4 + part, pl.ds(cols + col, 1), :]
            for r in range(rows):
                cell = pl.ds(r * cols + col, 1)
                packed[at, pl.ds(1 + rows * core + r, 1), :] = own[4 + part, cell, :]
                packed[at, pl.ds(1 + rows * (1 - core) + r, 1), :] = partner[4 + part, cell, :]
            packed[at, pl.ds(1 + 2 * rows, 1), :] = ring[4 + part, pl.ds(col, 1), :]
    packed[10:13] = ring[4:7]


def final_kernel(
    rows, cols, cell_count, place, offsets, counts, own, x_table, y_table, last,
    near_a, near_b, near_c, near_d, near_e, velocity, moved, near, far, turned,
):
    cells = rows * cols
    slots = own.shape[2]
    core = place[2]
    shape = (HALF, 2 * MODES)
    lane = lax.broadcasted_iota(jnp.int32, shape, 1)
    m = lax.broadcasted_iota(jnp.int32, shape, 0).astype(jnp.float32)
    n = (lane & (HALF - 1)).astype(jnp.float32)
    square = (two_pi * two_pi) * (m * m + n * n)
    keep = square > 0.0
    safe = jnp.where(keep, square, 1.0)
    damping = jnp.where(keep, jnp.exp(-safe / (6.25 * cell_count * cell_count)) / safe, 0.0)
    damping = damping * (4.0 * two_pi)
    u_weight = damping * n * jnp.where(m == 0.0, 0.5, 1.0)
    v_weight = damping * m * jnp.where(n == 0.0, 0.5, 1.0)
    total = last[0:4].reshape(shape)
    y_odd = (lane & HALF) != 0
    swapped = jnp.where(y_odd, -pltpu.roll(total, HALF, 1), pltpu.roll(total, 2 * MODES - HALF, 1))
    u_part = u_weight * swapped
    crossed = pltpu.roll(total, MODES, 1)
    v_part = v_weight * jnp.where(lane < MODES, -crossed, crossed)
    left = []
    for part in (u_part, v_part):
        other = pltpu.roll(part, MODES, 1)
        for doubled in (
            jnp.where(lane < MODES, part, other),
            jnp.where(lane < MODES, other, part),
        ):
            left.append(jnp.concatenate(split(doubled), axis=1))
    left = jnp.concatenate(left, axis=0)
    right = jnp.concatenate([y_table[...], y_table[...]], axis=0)
    terms = jnp.dot(left, right, preferred_element_type=jnp.float32)
    for i in range(cells):
        lanes = slice(i * slots, (i + 1) * slots)
        wave = x_table[:, lanes]
        far[0, pl.ds(i, 1), :] = jnp.sum(terms[0:MODES, lanes] * wave, axis=0, keepdims=True)
        far[1, pl.ds(i, 1), :] = jnp.sum(terms[MODES:, lanes] * wave, axis=0, keepdims=True)
    near[...] = (near_a[...] + near_b[...]) + (near_c[...] + near_d[...]) + near_e[...]
    near_cols(rows, cols, own, last, 4, core, lax.rem(place[1], 2), near, turned)
    live = count_grid(counts, rows, cols, (cells, slots))
    for part in range(2):
        value = jnp.where(live, near[part] + far[part], 0.0)
        for r in range(rows):
            piece = value[r * cols : (r + 1) * cols]
            velocity[part, r] = piece
            moved[part, r] = offsets[part, r] + section_step * piece


def far_item(items, index):
    count = 1 << (len(items) - 1)
    up = jnp.where(index % 2 == 1, (index + 1) % count, (index + count - 1) % count)
    mask = index ^ up
    chosen = items[-1]
    for k in range(2, len(items) - 1):
        chosen = jnp.where(mask == (1 << k) - 1, items[k], chosen)
    return chosen


def per_device(offsets, circ, counts):
    rows, cols, slots = circ.shape
    cells = rows * cols
    tx_size, ty_size = lax.axis_size("tx"), lax.axis_size("ty")
    chips = tx_size // 2
    cell_count = rows * tx_size
    tx, ty = lax.axis_index("tx"), lax.axis_index("ty")
    core, chip = tx % 2, tx // 2
    place = jnp.stack([tx, ty, core]).astype(jnp.int32)
    f32, bf16 = jnp.float32, jnp.bfloat16
    turned = [pltpu.VMEM((slots, 128), f32)]
    near_shape = [((2, cells, slots), f32)]

    own, x_table, y_table = call(
        functools.partial(moments_kernel, rows, cols, cell_count),
        [((7, cells, slots), f32), ((MODES, cells * slots), f32), ((2 * MODES, cells * slots), bf16)],
        [pltpu.VMEM((2, 5, 3, cells, slots), f32), pltpu.VMEM((2 * MODES, cells * slots), bf16)],
        4_000_000,
        place, offsets, counts, circ,
    )

    def swap(message, chip_bit, column_bit):
        pairs = [
            (i * ty_size + q, ((i // 2 ^ chip_bit) * 2 + (i + 1) % 2) * ty_size + (q ^ column_bit))
            for i in range(tx_size)
            for q in range(ty_size)
        ]
        return lax.ppermute(message, ("tx", "ty"), pairs)

    def near_call(body, flops, *args):
        return call(body, near_shape, turned, flops, *args)[0]

    whole = [(r, c) for c in range(cols) for r in range(rows)]
    third = len(whole) // 4
    partner = swap(own, 0, 0)
    near_a = near_call(
        functools.partial(near_local_kernel, rows, cols, whole[:third]), 4_000_000, own
    )
    total = own[0:4] + partner[0:4]
    first = jnp.where(core == 0, own[4:7], partner[4:7])
    second = jnp.where(core == 0, partner[4:7], own[4:7])
    items = [jnp.concatenate([first[:, 0:cols], second[:, cells - cols : cells]], axis=1)]
    bit = 1
    while bit < chips:
        message = jnp.concatenate([total, items[-1]], axis=0)
        got = swap(message, bit, 0)
        total = total + got[0:4]
        items.append(got[4:7])
        bit *= 2
    near_b = near_call(
        functools.partial(near_local_kernel, rows, cols, whole[third : 3 * third]), 9_000_000, own
    )
    near_c = near_call(
        functools.partial(near_partner_kernel, rows, cols, whole[3 * third :]), 9_000_000,
        place, own, partner,
    )
    slot_of = lax.broadcasted_iota(jnp.int32, (3, 2 * cols, slots), 1)
    below = slot_of < cols
    distant = far_item(items, chip) if chips > 2 else items[1]
    ring = jnp.where(below == (chip % 2 == 0), items[1], distant)
    shift = jnp.where(below, 2.0 * rows * unit, -2.0 * rows * unit)
    which = lax.broadcasted_iota(jnp.int32, (3, 2 * cols, slots), 0)
    ring = ring + jnp.where(which == 1, shift, 0.0)
    (packed,) = call(
        functools.partial(pack_kernel, rows, cols), [((13, cells, slots), f32)], [], 100_000,
        place, own, partner, jnp.concatenate([total, ring], axis=0),
    )
    got = swap(packed, 0, 1)
    near_d = near_call(
        functools.partial(near_ring_kernel, rows, cols), 5_000_000, place, own, packed
    )
    total = packed[0:4] + got[0:4]
    close = jnp.where(ty % 2 == 0, got[4:7], got[7:10])
    items = [None, jnp.where(ty % 2 == 0, got[7:10], got[4:7])]
    bit = 2
    while bit < ty_size:
        message = jnp.concatenate([total, items[-1]], axis=0)
        got = swap(message, 0, bit)
        total = total + got[0:4]
        items.append(got[4:7])
        bit *= 2
    near_e = near_call(
        functools.partial(near_close_kernel, rows, cols), 3_000_000, place, own, close
    )
    distant = far_item(items, ty) if ty_size > 2 else items[1]
    last = jnp.concatenate([total, distant], axis=0)
    return tuple(
        call(
            functools.partial(final_kernel, rows, cols, cell_count),
            [(offsets.shape, f32)] * 2,
            [pltpu.VMEM((2, cells, slots), f32), pltpu.VMEM((2, cells, slots), f32)] + turned,
            4_000_000,
            place, offsets, counts, own, x_table, y_table, last,
            near_a, near_b, near_c, near_d, near_e,
        )
    )


def solution(mesh):
    placed = (P(None, "tx", "ty", None), P("tx", "ty", None), P("tx", "ty"))

    return jax.shard_map(
        per_device,
        mesh=mesh,
        in_specs=placed,
        out_specs=(P(None, "tx", "ty", None), P(None, "tx", "ty", None)),
        check_vma=False,
    )
```

```python
import functools
import math

import jax
import jax.numpy as jnp
from jax import lax
from jax.experimental import pallas as pl
from jax.experimental.pallas import tpu as pltpu
from jax.sharding import PartitionSpec as P


MODES = 64
HALF = MODES // 2

two_pi = 2.0 * math.pi
screen = 1.5625
smooth = 0.0625
section_step = 0.25
unit = math.sqrt(screen / math.log(2.0))
floor_term = smooth * unit * unit

VMEM = pl.BlockSpec(memory_space=pltpu.VMEM)
PARAMS = pltpu.CompilerParams(vmem_limit_bytes=8 * 1024 * 1024)


def position():
    tx = lax.axis_index("tx")
    return tx, lax.axis_index("ty"), lax.rem(tx, 2)


def call(body, out_shapes, scratch, flops, *args):
    outs = [jax.ShapeDtypeStruct(s, d) for s, d in out_shapes]
    return pl.pallas_call(
        body,
        out_shape=outs,
        in_specs=[VMEM] * len(args),
        out_specs=[VMEM] * len(outs),
        scratch_shapes=scratch,
        compiler_params=PARAMS,
        cost_estimate=pl.CostEstimate(flops=flops, bytes_accessed=65536, transcendentals=0),
    )(*args)


def unit_circle(turn):
    quarter = jnp.floor(4.0 * turn + 0.5)
    angle = two_pi * (turn - 0.25 * quarter)
    sq = angle * angle
    sine = angle * (
        1.0 + sq * (-1.0 / 6 + sq * (1.0 / 120 + sq * (-1.0 / 5040 + sq * (1.0 / 362880))))
    )
    cosine = 1.0 + sq * (
        -0.5 + sq * (1.0 / 24 + sq * (-1.0 / 720 + sq * (1.0 / 40320 + sq * (-1.0 / 3628800))))
    )
    odd = (quarter == 1.0) | (quarter == 3.0)
    cos_neg = (quarter == 1.0) | (quarter == 2.0)
    sin_neg = (quarter == 2.0) | (quarter == 3.0)
    cos_part = jnp.where(odd, sine, cosine)
    sin_part = jnp.where(odd, cosine, sine)
    return jnp.where(cos_neg, -cos_part, cos_part), jnp.where(sin_neg, -sin_part, sin_part)


def times(p, q):
    return p[0] * q[0] - p[1] * q[1], p[0] * q[1] + p[1] * q[0]


def split(value):
    high = value.astype(jnp.bfloat16)
    low = (value - high.astype(jnp.float32)).astype(jnp.bfloat16)
    return high, low


def moments_kernel(
    rows, cols, cell_count, slot_state, own, kept, x_table, y_table, powers, weighted
):
    cells = rows * cols
    slots = slot_state.shape[3]
    shape = (cells, slots)
    place = position()
    cell = lax.broadcasted_iota(jnp.int32, shape, 0)
    row_in = jnp.zeros(shape, jnp.int32)
    for r in range(1, rows):
        row_in = jnp.where(cell >= r * cols, r, row_in)
    col_in = cell - row_in * cols
    for part in range(4):
        for r in range(rows):
            kept[part, pl.ds(r * cols, cols), :] = slot_state[part, r]
    off_x, off_y, strength = kept[0], kept[1], kept[2]
    x_turn = ((place[1] * cols + col_in).astype(jnp.float32) + off_x) / cell_count
    y_turn = ((place[0] * rows + row_in).astype(jnp.float32) + off_y) / cell_count
    own[4] = unit * (col_in.astype(jnp.float32) + off_x)
    own[5] = unit * ((place[2] * rows + row_in).astype(jnp.float32) + off_y)
    own[6] = strength * (unit * cell_count / two_pi)
    for axis, turn in ((0, x_turn), (1, y_turn)):
        point = unit_circle(turn)
        for power in range(5):
            powers[axis, power, 0] = point[0]
            powers[axis, power, 1] = point[1]
            if power < 4:
                point = times(point, point)
    powers[0, 0, 2] = strength
    mode = lax.broadcasted_iota(jnp.int32, (8, slots), 0)
    bits = [(mode & (1 << b)) != 0 for b in range(3)]
    for i in range(cells):
        lanes = pl.ds(i * slots, slots)
        amount = jnp.broadcast_to(powers[0, 0, 2, pl.ds(i, 1), :], (8, slots))
        for axis in range(2):

            def row(power, part):
                return jnp.broadcast_to(powers[axis, power, part, pl.ds(i, 1), :], (8, slots))

            group = None
            for b in range(3):
                factor = (jnp.where(bits[b], row(b, 0), 1.0), jnp.where(bits[b], row(b, 1), 0.0))
                group = factor if group is None else times(group, factor)
            eight = (row(3, 0), row(3, 1))
            sixteen = (row(4, 0), row(4, 1))
            second = times(group, eight)
            groups = [group, second, times(group, sixteen), times(second, sixteen)]
            wave = jnp.concatenate([g[0] for g in groups] + [g[1] for g in groups], axis=0)
            if axis == 0:
                x_table[:, lanes] = wave
                high, low = split(wave * jnp.concatenate([amount] * 8, axis=0))
                weighted[0:MODES, lanes] = high
                weighted[MODES : 2 * MODES, lanes] = low
            else:
                high, low = split(wave)
                y_table[0:MODES, lanes] = high
                y_table[MODES : 2 * MODES, lanes] = low
    full = lax.dot_general(
        weighted[...],
        y_table[...],
        (((1,), (1,)), ((), ())),
        preferred_element_type=jnp.float32,
    )
    full = full[0:MODES] + full[MODES : 2 * MODES]
    full = full + pltpu.roll(full, MODES, 1)
    lane = lax.broadcasted_iota(jnp.int32, (HALF, 2 * MODES), 1)
    own[0:4] = jnp.where(lane < MODES, full[0:HALF], full[HALF:MODES]).reshape(4, 8, 2 * MODES)


def pair_terms(target, source, total):
    offset_x = target[0] - source[0]
    offset_y = target[1] - source[1]
    square = offset_x * offset_x + offset_y * offset_y
    weight = source[2] / ((square + floor_term) * jnp.exp2(square))
    return total[0] - offset_y * weight, total[1] + offset_x * weight


def near_sum(sources, targets, links, turned):
    slots = sources[0][0].shape[1]
    stack = [part for source in sources for part in source]
    pad = -len(stack) % 8
    stack = jnp.concatenate(stack + [jnp.zeros((pad, slots), jnp.float32)] * (pad > 0), axis=0)
    turned[:, 0 : stack.shape[0]] = stack.T
    spread = [tuple(jnp.broadcast_to(part, (8, slots)) for part in t) for t in targets]

    def step(k, totals):
        totals = list(totals)
        chunk = turned[pl.ds(pl.multiple_of(8 * k, 8), 8), :]
        for i, reached in enumerate(links):
            source = tuple(
                jnp.broadcast_to(chunk[:, 3 * i + part : 3 * i + part + 1], (8, slots))
                for part in range(3)
            )
            for t in reached:
                totals[2 * t], totals[2 * t + 1] = pair_terms(
                    spread[t], source, (totals[2 * t], totals[2 * t + 1])
                )
        return tuple(totals)

    zero = jnp.zeros((8, slots), jnp.float32)
    pairs = sum(len(reached) for reached in links)
    chunks = slots // 8
    group = 1
    while group * 2 * pairs <= 48 and chunks % (group * 2) == 0:
        group *= 2

    def grouped(k, totals):
        for u in range(group):
            totals = step(k * group + u, totals)
        return totals

    totals = lax.fori_loop(0, chunks // group, grouped, (zero,) * (2 * len(targets)))
    return [jnp.sum(total, axis=0, keepdims=True) for total in totals]


def reach(col, cols):
    return [c for c in (col - 1, col, col + 1) if 0 <= c < cols]


def read_row(ref, base, at):
    return tuple(ref[base + part, pl.ds(at, 1), :] for part in range(3))


def near_local(rows, cols, own, cells, near, turned):
    places = sorted({(r, c) for row, col in cells for r in range(rows) if abs(r - row) <= 1 for c in reach(col, cols)})
    sources = [read_row(own, 4, r * cols + c) for r, c in cells]
    targets = [read_row(own, 4, r * cols + c)[:2] for r, c in places]
    links = [
        [t for t, (r, c) in enumerate(places) if abs(r - row) <= 1 and abs(c - col) <= 1]
        for row, col in cells
    ]
    sums = near_sum(sources, targets, links, turned)
    for t, (r, c) in enumerate(places):
        for part in range(2):
            at = pl.ds(r * cols + c, 1)
            near[part, at, :] = near[part, at, :] + sums[2 * t + part]


def near_local_kernel(rows, cols, cells, own, near, turned):
    near[...] = jnp.zeros_like(near)
    near_local(rows, cols, own, cells, near, turned)


def near_rows(rows, cols, own, outer, base, above, near, turned):
    def pick(ref, origin, part, first, second):
        return jnp.where(
            above == 1, ref[origin + part, pl.ds(first, 1), :], ref[origin + part, pl.ds(second, 1), :]
        )

    sources = [
        tuple(pick(outer, base, part, cols + c, c) for part in range(3)) for c in range(cols)
    ]
    last = (rows - 1) * cols
    targets = [tuple(pick(own, 4, part, c, last + c) for part in range(2)) for c in range(cols)]
    sums = near_sum(sources, targets, [reach(c, cols) for c in range(cols)], turned)
    top = jnp.where(above == 1, 0, last)
    for c in range(cols):
        for part in range(2):
            at = pl.ds(top + c, 1)
            near[part, at, :] = near[part, at, :] + sums[2 * c + part]


def near_cols(rows, cols, own, side, base, core, right, near, turned):
    shift = jnp.where(right == 1, unit * cols, -unit * cols)
    sources = []
    for k in range(rows + 2):
        row = read_row(side, base, core * rows + k)
        sources.append((row[0] + shift, row[1], row[2]))
    edge = jnp.where(right == 1, cols - 1, 0)
    targets = [read_row(own, 4, r * cols + edge)[:2] for r in range(rows)]
    links = [[r for r in range(rows) if 0 <= k - r <= 2] for k in range(rows + 2)]
    sums = near_sum(sources, targets, links, turned)
    for r in range(rows):
        for part in range(2):
            at = pl.ds(r * cols + edge, 1)
            near[part, at, :] = near[part, at, :] + sums[2 * r + part]


def near_partner_kernel(rows, cols, cells, own, partner, near, turned):
    place = position()
    near[...] = jnp.zeros_like(near)
    near_local(rows, cols, own, cells, near, turned)
    near_rows(rows, cols, own, partner, 4, place[2], near, turned)


def near_ring_kernel(rows, cols, own, ring, near, turned):
    place = position()
    near[...] = jnp.zeros_like(near)
    near_rows(rows, cols, own, ring, 0, 1 - place[2], near, turned)


def near_close_kernel(rows, cols, cell_count, own, close, near, weights, turned):
    shape = (HALF, 2 * MODES)
    lane = lax.broadcasted_iota(jnp.int32, shape, 1)
    m = lax.broadcasted_iota(jnp.int32, shape, 0).astype(jnp.float32)
    n = (lane & (HALF - 1)).astype(jnp.float32)
    square = (two_pi * two_pi) * (m * m + n * n)
    keep = square > 0.0
    safe = jnp.where(keep, square, 1.0)
    damping = jnp.where(keep, jnp.exp(-safe / (6.25 * cell_count * cell_count)) / safe, 0.0)
    damping = damping * (4.0 * two_pi)
    u_weight = damping * n * jnp.where(m == 0.0, 0.5, 1.0)
    v_weight = damping * m * jnp.where(n == 0.0, 0.5, 1.0)
    weights[0] = u_weight
    weights[1] = v_weight
    place = position()
    near[...] = jnp.zeros_like(near)
    right = 1 - lax.rem(place[1], 2)
    near_cols(rows, cols, own, close, 0, place[2], right, near, turned)


def pack_kernel(rows, cols, own, partner, ring, packed, ring_out):
    core = position()[2]
    packed[4:10] = jnp.zeros((6,) + packed.shape[1:], jnp.float32)
    packed[0:4] = ring[0:4]
    for edge, col in ((0, 0), (1, cols - 1)):
        for part in range(3):
            at = 4 + 3 * edge + part
            packed[at, pl.ds(0, 1), :] = ring[4 + part, pl.ds(cols + col, 1), :]
            for r in range(rows):
                cell = pl.ds(r * cols + col, 1)
                packed[at, pl.ds(1 + rows * core + r, 1), :] = own[4 + part, cell, :]
                packed[at, pl.ds(1 + rows * (1 - core) + r, 1), :] = partner[4 + part, cell, :]
            packed[at, pl.ds(1 + 2 * rows, 1), :] = ring[4 + part, pl.ds(col, 1), :]
    ring_out[...] = ring[4:7]


def final_kernel(
    rows, cols, kept, own, x_table, y_table, last,
    near_a, near_b, near_c, near_d, near_e, weights, velocity, moved, near, far, turned,
):
    cells = rows * cols
    slots = own.shape[2]
    place = position()
    core = place[2]
    shape = (HALF, 2 * MODES)
    lane = lax.broadcasted_iota(jnp.int32, shape, 1)
    total = last[0:4].reshape(shape)
    y_odd = (lane & HALF) != 0
    swapped = jnp.where(y_odd, -pltpu.roll(total, HALF, 1), pltpu.roll(total, 2 * MODES - HALF, 1))
    u_part = weights[0] * swapped
    crossed = pltpu.roll(total, MODES, 1)
    v_part = weights[1] * jnp.where(lane < MODES, -crossed, crossed)
    left = []
    for part in (u_part, v_part):
        other = pltpu.roll(part, MODES, 1)
        for doubled in (
            jnp.where(lane < MODES, part, other),
            jnp.where(lane < MODES, other, part),
        ):
            left.append(jnp.concatenate(split(doubled), axis=1))
    left = jnp.concatenate(left, axis=0)
    right = jnp.concatenate([y_table[...], y_table[...]], axis=0)
    terms = jnp.dot(left, right, preferred_element_type=jnp.float32)
    for i in range(cells):
        lanes = slice(i * slots, (i + 1) * slots)
        wave = x_table[:, lanes]
        far[0, pl.ds(i, 1), :] = jnp.sum(terms[0:MODES, lanes] * wave, axis=0, keepdims=True)
        far[1, pl.ds(i, 1), :] = jnp.sum(terms[MODES:, lanes] * wave, axis=0, keepdims=True)
    near[...] = (near_a[...] + near_b[...]) + (near_c[...] + near_d[...]) + near_e[...]
    near_cols(rows, cols, own, last, 4, core, lax.rem(place[1], 2), near, turned)
    live = kept[3] > 0.5
    for part in range(2):
        value = jnp.where(live, near[part] + far[part], 0.0)
        after = kept[part] + section_step * value
        for r in range(rows):
            velocity[part, r] = value[r * cols : (r + 1) * cols]
            moved[part, r] = after[r * cols : (r + 1) * cols]


def far_item(items, index):
    count = 1 << (len(items) - 1)
    up = jnp.where(index % 2 == 1, (index + 1) % count, (index + count - 1) % count)
    mask = index ^ up
    chosen = items[-1]
    for k in range(2, len(items) - 1):
        chosen = jnp.where(mask == (1 << k) - 1, items[k], chosen)
    return chosen


def per_device(offsets, circ, counts):
    rows, cols, slots = circ.shape
    cells = rows * cols
    tx_size, ty_size = lax.axis_size("tx"), lax.axis_size("ty")
    chips = tx_size // 2
    cell_count = rows * tx_size
    tx, ty = lax.axis_index("tx"), lax.axis_index("ty")
    core, chip = tx % 2, tx // 2
    f32, bf16 = jnp.float32, jnp.bfloat16
    turned = [pltpu.VMEM((slots, 128), f32)]
    near_shape = [((2, cells, slots), f32)]

    live = lax.broadcasted_iota(jnp.int32, circ.shape, 2) < counts[:, :, None]
    slot_state = jnp.stack(
        [offsets[0], offsets[1], jnp.where(live, circ, 0.0), jnp.where(live, 1.0, 0.0)]
    )
    own, kept, x_table, y_table = call(
        functools.partial(moments_kernel, rows, cols, cell_count),
        [
            ((7, cells, slots), f32),
            ((4, cells, slots), f32),
            ((MODES, cells * slots), f32),
            ((2 * MODES, cells * slots), bf16),
        ],
        [
            pltpu.VMEM((2, 5, 3, cells, slots), f32),
            pltpu.VMEM((2 * MODES, cells * slots), bf16),
        ],
        4_000_000,
        slot_state,
    )

    def swap(message, chip_bit, column_bit):
        pairs = [
            (i * ty_size + q, ((i // 2 ^ chip_bit) * 2 + (i + 1) % 2) * ty_size + (q ^ column_bit))
            for i in range(tx_size)
            for q in range(ty_size)
        ]
        return lax.ppermute(message, ("tx", "ty"), pairs)

    def near_call(body, flops, *args):
        return call(body, near_shape, turned, flops, *args)[0]

    whole = [(r, c) for c in range(cols) for r in range(rows)]
    third = len(whole) // 4
    partner = swap(own, 0, 0)
    near_a = near_call(
        functools.partial(near_local_kernel, rows, cols, whole[:third]), 4_000_000, own
    )
    total = own[0:4] + partner[0:4]
    first = jnp.where(core == 0, own[4:7], partner[4:7])
    second = jnp.where(core == 0, partner[4:7], own[4:7])
    items = [jnp.concatenate([first[:, 0:cols], second[:, cells - cols : cells]], axis=1)]
    bit = 1
    while bit < chips:
        message = jnp.concatenate([total, items[-1]], axis=0)
        got = swap(message, bit, 0)
        total = total + got[0:4]
        items.append(got[4:7])
        bit *= 2
    near_b = near_call(
        functools.partial(near_local_kernel, rows, cols, whole[third : 3 * third]), 9_000_000, own
    )
    near_c = near_call(
        functools.partial(near_partner_kernel, rows, cols, whole[3 * third :]), 9_000_000,
        own, partner,
    )
    slot_of = lax.broadcasted_iota(jnp.int32, (3, 2 * cols, slots), 1)
    below = slot_of < cols
    distant = far_item(items, chip) if chips > 2 else items[1]
    ring = jnp.where(below == (chip % 2 == 0), items[1], distant)
    shift = jnp.where(below, 2.0 * rows * unit, -2.0 * rows * unit)
    which = lax.broadcasted_iota(jnp.int32, (3, 2 * cols, slots), 0)
    ring = ring + jnp.where(which == 1, shift, 0.0)
    packed, ring = call(
        functools.partial(pack_kernel, rows, cols),
        [((10, cells, slots), f32), ((3, 2 * cols, slots), f32)], [], 100_000,
        own, partner, jnp.concatenate([total, ring], axis=0),
    )
    got = swap(packed, 0, 1)
    near_d = near_call(functools.partial(near_ring_kernel, rows, cols), 5_000_000, own, ring)
    total = packed[0:4] + got[0:4]
    close = jnp.where(ty % 2 == 0, got[4:7], got[7:10])
    items = [None, jnp.where(ty % 2 == 0, got[7:10], got[4:7])]
    bit = 2
    while bit < ty_size:
        message = jnp.concatenate([total, items[-1]], axis=0)
        got = swap(message, 0, bit)
        total = total + got[0:4]
        items.append(got[4:7])
        bit *= 2
    near_e, weights = call(
        functools.partial(near_close_kernel, rows, cols, cell_count),
        near_shape + [((2, HALF, 2 * MODES), f32)], turned, 3_000_000,
        own, close,
    )
    distant = far_item(items, ty) if ty_size > 2 else items[1]
    last = jnp.concatenate([total, distant], axis=0)
    return tuple(
        call(
            functools.partial(final_kernel, rows, cols),
            [(offsets.shape, f32)] * 2,
            [pltpu.VMEM((2, cells, slots), f32), pltpu.VMEM((2, cells, slots), f32)] + turned,
            4_000_000,
            kept, own, x_table, y_table, last,
            near_a, near_b, near_c, near_d, near_e, weights,
        )
    )


def solution(mesh):
    placed = (P(None, "tx", "ty", None), P("tx", "ty", None), P("tx", "ty"))

    return jax.shard_map(
        per_device,
        mesh=mesh,
        in_specs=placed,
        out_specs=(P(None, "tx", "ty", None), P(None, "tx", "ty", None)),
        check_vma=False,
    )
```

```python
import functools
import math

import jax
import jax.numpy as jnp
from jax import lax
from jax.experimental import pallas as pl
from jax.experimental.pallas import tpu as pltpu
from jax.sharding import PartitionSpec as P


MODES = 64
HALF = MODES // 2

two_pi = 2.0 * math.pi
screen = 1.5625
smooth = 0.0625
section_step = 0.25
unit = math.sqrt(screen / math.log(2.0))
floor_term = smooth * unit * unit

VMEM = pl.BlockSpec(memory_space=pltpu.VMEM)
PARAMS = pltpu.CompilerParams(vmem_limit_bytes=8 * 1024 * 1024)


def position():
    tx = lax.axis_index("tx")
    return tx, lax.axis_index("ty"), lax.rem(tx, 2)


def call(body, out_shapes, scratch, flops, *args):
    outs = [jax.ShapeDtypeStruct(s, d) for s, d in out_shapes]
    return pl.pallas_call(
        body,
        out_shape=outs,
        in_specs=[VMEM] * len(args),
        out_specs=[VMEM] * len(outs),
        scratch_shapes=scratch,
        compiler_params=PARAMS,
        cost_estimate=pl.CostEstimate(flops=flops, bytes_accessed=65536, transcendentals=0),
    )(*args)


def unit_circle(turn):
    quarter = jnp.floor(4.0 * turn + 0.5)
    angle = two_pi * (turn - 0.25 * quarter)
    sq = angle * angle
    sine = angle * (
        1.0 + sq * (-1.0 / 6 + sq * (1.0 / 120 + sq * (-1.0 / 5040 + sq * (1.0 / 362880))))
    )
    cosine = 1.0 + sq * (
        -0.5 + sq * (1.0 / 24 + sq * (-1.0 / 720 + sq * (1.0 / 40320 + sq * (-1.0 / 3628800))))
    )
    odd = (quarter == 1.0) | (quarter == 3.0)
    cos_neg = (quarter == 1.0) | (quarter == 2.0)
    sin_neg = (quarter == 2.0) | (quarter == 3.0)
    cos_part = jnp.where(odd, sine, cosine)
    sin_part = jnp.where(odd, cosine, sine)
    return jnp.where(cos_neg, -cos_part, cos_part), jnp.where(sin_neg, -sin_part, sin_part)


def times(p, q):
    return p[0] * q[0] - p[1] * q[1], p[0] * q[1] + p[1] * q[0]


def split(value):
    high = value.astype(jnp.bfloat16)
    low = (value - high.astype(jnp.float32)).astype(jnp.bfloat16)
    return high, low


def moments_kernel(
    rows, cols, cell_count, slot_state, own, kept, x_table, y_table, powers, weighted
):
    cells = rows * cols
    slots = slot_state.shape[3]
    shape = (cells, slots)
    place = position()
    cell = lax.broadcasted_iota(jnp.int32, shape, 0)
    row_in = jnp.zeros(shape, jnp.int32)
    for r in range(1, rows):
        row_in = jnp.where(cell >= r * cols, r, row_in)
    col_in = cell - row_in * cols
    for part in range(4):
        for r in range(rows):
            kept[part, pl.ds(r * cols, cols), :] = slot_state[part, r]
    off_x, off_y, strength = kept[0], kept[1], kept[2]
    x_turn = ((place[1] * cols + col_in).astype(jnp.float32) + off_x) / cell_count
    y_turn = ((place[0] * rows + row_in).astype(jnp.float32) + off_y) / cell_count
    own[4] = unit * (col_in.astype(jnp.float32) + off_x)
    own[5] = unit * ((place[2] * rows + row_in).astype(jnp.float32) + off_y)
    own[6] = strength * (unit * cell_count / two_pi)
    for axis, turn in ((0, x_turn), (1, y_turn)):
        point = unit_circle(turn)
        for power in range(5):
            powers[axis, power, 0] = point[0]
            powers[axis, power, 1] = point[1]
            if power < 4:
                point = times(point, point)
    powers[0, 0, 2] = strength
    mode = lax.broadcasted_iota(jnp.int32, (8, slots), 0)
    bits = [(mode & (1 << b)) != 0 for b in range(3)]
    for i in range(cells):
        lanes = pl.ds(i * slots, slots)
        amount = jnp.broadcast_to(powers[0, 0, 2, pl.ds(i, 1), :], (8, slots))
        for axis in range(2):

            def row(power, part):
                return jnp.broadcast_to(powers[axis, power, part, pl.ds(i, 1), :], (8, slots))

            group = None
            for b in range(3):
                factor = (jnp.where(bits[b], row(b, 0), 1.0), jnp.where(bits[b], row(b, 1), 0.0))
                group = factor if group is None else times(group, factor)
            eight = (row(3, 0), row(3, 1))
            sixteen = (row(4, 0), row(4, 1))
            second = times(group, eight)
            groups = [group, second, times(group, sixteen), times(second, sixteen)]
            wave = jnp.concatenate([g[0] for g in groups] + [g[1] for g in groups], axis=0)
            if axis == 0:
                x_table[:, lanes] = wave
                high, low = split(wave * jnp.concatenate([amount] * 8, axis=0))
                weighted[0:MODES, lanes] = high
                weighted[MODES : 2 * MODES, lanes] = low
            else:
                high, low = split(wave)
                y_table[0:MODES, lanes] = high
                y_table[MODES : 2 * MODES, lanes] = low
    full = lax.dot_general(
        weighted[...],
        y_table[...],
        (((1,), (1,)), ((), ())),
        preferred_element_type=jnp.float32,
    )
    full = full[0:MODES] + full[MODES : 2 * MODES]
    full = full + pltpu.roll(full, MODES, 1)
    lane = lax.broadcasted_iota(jnp.int32, (HALF, 2 * MODES), 1)
    own[0:4] = jnp.where(lane < MODES, full[0:HALF], full[HALF:MODES]).reshape(4, 8, 2 * MODES)


def pair_terms(target, source, total):
    offset_x = target[0] - source[0]
    offset_y = target[1] - source[1]
    square = offset_x * offset_x + offset_y * offset_y
    weight = source[2] / ((square + floor_term) * jnp.exp2(square))
    return total[0] - offset_y * weight, total[1] + offset_x * weight


def near_sum(sources, targets, links, turned, most=48):
    slots = sources[0][0].shape[1]
    stack = [part for source in sources for part in source]
    pad = -len(stack) % 8
    stack = jnp.concatenate(stack + [jnp.zeros((pad, slots), jnp.float32)] * (pad > 0), axis=0)
    turned[:, 0 : stack.shape[0]] = stack.T
    spread = [tuple(jnp.broadcast_to(part, (8, slots)) for part in t) for t in targets]

    def step(k, totals):
        totals = list(totals)
        chunk = turned[pl.ds(8 * k if isinstance(k, int) else pl.multiple_of(8 * k, 8), 8), :]
        for i, reached in enumerate(links):
            source = tuple(
                jnp.broadcast_to(chunk[:, 3 * i + part : 3 * i + part + 1], (8, slots))
                for part in range(3)
            )
            for t in reached:
                totals[2 * t], totals[2 * t + 1] = pair_terms(
                    spread[t], source, (totals[2 * t], totals[2 * t + 1])
                )
        return tuple(totals)

    zero = jnp.zeros((8, slots), jnp.float32)
    pairs = sum(len(reached) for reached in links)
    chunks = slots // 8
    group = 1
    while group * 2 * pairs <= most and chunks % (group * 2) == 0:
        group *= 2

    def grouped(k, totals):
        for u in range(group):
            totals = step(k * group + u, totals)
        return totals

    totals = (zero,) * (2 * len(targets))
    if group == chunks:
        totals = grouped(0, totals)
    else:
        totals = lax.fori_loop(0, chunks // group, grouped, totals)
    return [jnp.sum(total, axis=0, keepdims=True) for total in totals]


def reach(col, cols):
    return [c for c in (col - 1, col, col + 1) if 0 <= c < cols]


def read_row(ref, base, at):
    return tuple(ref[base + part, pl.ds(at, 1), :] for part in range(3))


def near_last_cols(rows, cols, side, spread, core, right, near):
    slots = side.shape[2]
    shift = jnp.where(right == 1, unit * cols, -unit * cols)
    sources = []
    for k in range(rows + 2):
        row = read_row(side, 4, core * rows + k)
        row = (row[0] + shift, row[1], row[2])
        sources.append(tuple(jnp.broadcast_to(part, (8, slots)) for part in row))
    stack = []
    for r in range(rows):
        parts = ([], [])
        for k in range(slots // 8):
            target = tuple(spread[2 * r + part, 8 * k : 8 * k + 8] for part in range(2))
            total = (0.0, 0.0)
            for i in range(r, r + 3):
                total = pair_terms(target, sources[i], total)
            parts[0].append(total[0])
            parts[1].append(total[1])
        stack += parts[0] + parts[1]
    high, low = split(jnp.concatenate(stack, axis=0))
    ones = jnp.ones((8, slots), jnp.bfloat16)

    def lanes_sum(value):
        return lax.dot_general(
            ones, value, (((1,), (1,)), ((), ())), preferred_element_type=jnp.float32
        )

    sums = lanes_sum(high) + lanes_sum(low)
    edge = jnp.where(right == 1, cols - 1, 0)
    for r in range(rows):
        for part in range(2):
            at = pl.ds(r * cols + edge, 1)
            lanes = slice((2 * r + part) * slots, (2 * r + part + 1) * slots)
            near[part, at, :] = near[part, at, :] + sums[0:1, lanes]


def near_local(rows, cols, own, cells, near, turned):
    places = sorted({(r, c) for row, col in cells for r in range(rows) if abs(r - row) <= 1 for c in reach(col, cols)})
    sources = [read_row(own, 4, r * cols + c) for r, c in cells]
    targets = [read_row(own, 4, r * cols + c)[:2] for r, c in places]
    links = [
        [t for t, (r, c) in enumerate(places) if abs(r - row) <= 1 and abs(c - col) <= 1]
        for row, col in cells
    ]
    sums = near_sum(sources, targets, links, turned)
    for t, (r, c) in enumerate(places):
        for part in range(2):
            at = pl.ds(r * cols + c, 1)
            near[part, at, :] = near[part, at, :] + sums[2 * t + part]


def near_local_kernel(rows, cols, cells, own, near, turned):
    near[...] = jnp.zeros_like(near)
    near_local(rows, cols, own, cells, near, turned)


def near_rows(rows, cols, own, outer, base, above, near, turned):
    def pick(ref, origin, part, first, second):
        return jnp.where(
            above == 1, ref[origin + part, pl.ds(first, 1), :], ref[origin + part, pl.ds(second, 1), :]
        )

    sources = [
        tuple(pick(outer, base, part, cols + c, c) for part in range(3)) for c in range(cols)
    ]
    last = (rows - 1) * cols
    targets = [tuple(pick(own, 4, part, c, last + c) for part in range(2)) for c in range(cols)]
    sums = near_sum(sources, targets, [reach(c, cols) for c in range(cols)], turned)
    top = jnp.where(above == 1, 0, last)
    for c in range(cols):
        for part in range(2):
            at = pl.ds(top + c, 1)
            near[part, at, :] = near[part, at, :] + sums[2 * c + part]


def near_cols(rows, cols, own, side, base, core, right, near, turned, most=48):
    shift = jnp.where(right == 1, unit * cols, -unit * cols)
    sources = []
    for k in range(rows + 2):
        row = read_row(side, base, core * rows + k)
        sources.append((row[0] + shift, row[1], row[2]))
    edge = jnp.where(right == 1, cols - 1, 0)
    targets = [read_row(own, 4, r * cols + edge)[:2] for r in range(rows)]
    links = [[r for r in range(rows) if 0 <= k - r <= 2] for k in range(rows + 2)]
    sums = near_sum(sources, targets, links, turned, most)
    for r in range(rows):
        for part in range(2):
            at = pl.ds(r * cols + edge, 1)
            near[part, at, :] = near[part, at, :] + sums[2 * r + part]


def near_partner_kernel(rows, cols, cells, own, partner, near, turned):
    place = position()
    near[...] = jnp.zeros_like(near)
    near_local(rows, cols, own, cells, near, turned)
    near_rows(rows, cols, own, partner, 4, place[2], near, turned)


def near_ring_kernel(rows, cols, own, ring, near, turned):
    place = position()
    near[...] = jnp.zeros_like(near)
    near_rows(rows, cols, own, ring, 0, 1 - place[2], near, turned)


def near_close_kernel(rows, cols, cell_count, own, close, near, weights, spread, turned):
    shape = (HALF, 2 * MODES)
    lane = lax.broadcasted_iota(jnp.int32, shape, 1)
    m = lax.broadcasted_iota(jnp.int32, shape, 0).astype(jnp.float32)
    n = (lane & (HALF - 1)).astype(jnp.float32)
    square = (two_pi * two_pi) * (m * m + n * n)
    keep = square > 0.0
    safe = jnp.where(keep, square, 1.0)
    damping = jnp.where(keep, jnp.exp(-safe / (6.25 * cell_count * cell_count)) / safe, 0.0)
    damping = damping * (4.0 * two_pi)
    u_weight = damping * n * jnp.where(m == 0.0, 0.5, 1.0)
    v_weight = damping * m * jnp.where(n == 0.0, 0.5, 1.0)
    weights[0] = u_weight
    weights[1] = v_weight
    place = position()
    near[...] = jnp.zeros_like(near)
    right = 1 - lax.rem(place[1], 2)
    slots = own.shape[2]
    edge = jnp.where(right == 1, 0, cols - 1)
    for r in range(rows):
        for part in range(2):
            row = own[4 + part, pl.ds(r * cols + edge, 1), :]
            spread[2 * r + part] = jnp.broadcast_to(row, (slots, slots)).T
    near_cols(rows, cols, own, close, 0, place[2], right, near, turned)


def pack_kernel(rows, cols, own, partner, ring, packed, ring_out):
    core = position()[2]
    packed[4:10] = jnp.zeros((6,) + packed.shape[1:], jnp.float32)
    packed[0:4] = ring[0:4]
    for edge, col in ((0, 0), (1, cols - 1)):
        for part in range(3):
            at = 4 + 3 * edge + part
            packed[at, pl.ds(0, 1), :] = ring[4 + part, pl.ds(cols + col, 1), :]
            for r in range(rows):
                cell = pl.ds(r * cols + col, 1)
                packed[at, pl.ds(1 + rows * core + r, 1), :] = own[4 + part, cell, :]
                packed[at, pl.ds(1 + rows * (1 - core) + r, 1), :] = partner[4 + part, cell, :]
            packed[at, pl.ds(1 + 2 * rows, 1), :] = ring[4 + part, pl.ds(col, 1), :]
    ring_out[...] = ring[4:7]


def final_kernel(
    rows, cols, kept, own, x_table, y_table, last,
    near_a, near_b, near_c, near_d, near_e, weights, spread, velocity, moved, near, far,
):
    cells = rows * cols
    slots = own.shape[2]
    place = position()
    core = place[2]
    shape = (HALF, 2 * MODES)
    lane = lax.broadcasted_iota(jnp.int32, shape, 1)
    total = last[0:4].reshape(shape)
    y_odd = (lane & HALF) != 0
    swapped = jnp.where(y_odd, -pltpu.roll(total, HALF, 1), pltpu.roll(total, 2 * MODES - HALF, 1))
    u_part = weights[0] * swapped
    crossed = pltpu.roll(total, MODES, 1)
    v_part = weights[1] * jnp.where(lane < MODES, -crossed, crossed)
    left = []
    for part in (u_part, v_part):
        other = pltpu.roll(part, MODES, 1)
        for doubled in (
            jnp.where(lane < MODES, part, other),
            jnp.where(lane < MODES, other, part),
        ):
            left.append(jnp.concatenate(split(doubled), axis=1))
    left = jnp.concatenate(left, axis=0)
    right = jnp.concatenate([y_table[...], y_table[...]], axis=0)
    terms = jnp.dot(left, right, preferred_element_type=jnp.float32)
    for i in range(cells):
        lanes = slice(i * slots, (i + 1) * slots)
        wave = x_table[:, lanes]
        far[0, pl.ds(i, 1), :] = jnp.sum(terms[0:MODES, lanes] * wave, axis=0, keepdims=True)
        far[1, pl.ds(i, 1), :] = jnp.sum(terms[MODES:, lanes] * wave, axis=0, keepdims=True)
    near[...] = (near_a[...] + near_b[...]) + (near_c[...] + near_d[...]) + near_e[...]
    near_last_cols(rows, cols, last, spread, core, lax.rem(place[1], 2), near)
    live = kept[3] > 0.5
    for part in range(2):
        value = jnp.where(live, near[part] + far[part], 0.0)
        after = kept[part] + section_step * value
        for r in range(rows):
            velocity[part, r] = value[r * cols : (r + 1) * cols]
            moved[part, r] = after[r * cols : (r + 1) * cols]


def far_item(items, index):
    count = 1 << (len(items) - 1)
    up = jnp.where(index % 2 == 1, (index + 1) % count, (index + count - 1) % count)
    mask = index ^ up
    chosen = items[-1]
    for k in range(2, len(items) - 1):
        chosen = jnp.where(mask == (1 << k) - 1, items[k], chosen)
    return chosen


def per_device(offsets, circ, counts):
    rows, cols, slots = circ.shape
    cells = rows * cols
    tx_size, ty_size = lax.axis_size("tx"), lax.axis_size("ty")
    chips = tx_size // 2
    cell_count = rows * tx_size
    tx, ty = lax.axis_index("tx"), lax.axis_index("ty")
    core, chip = tx % 2, tx // 2
    f32, bf16 = jnp.float32, jnp.bfloat16
    turned = [pltpu.VMEM((slots, 128), f32)]
    near_shape = [((2, cells, slots), f32)]

    live = lax.broadcasted_iota(jnp.int32, circ.shape, 2) < counts[:, :, None]
    slot_state = jnp.stack(
        [offsets[0], offsets[1], jnp.where(live, circ, 0.0), jnp.where(live, 1.0, 0.0)]
    )
    own, kept, x_table, y_table = call(
        functools.partial(moments_kernel, rows, cols, cell_count),
        [
            ((7, cells, slots), f32),
            ((4, cells, slots), f32),
            ((MODES, cells * slots), f32),
            ((2 * MODES, cells * slots), bf16),
        ],
        [
            pltpu.VMEM((2, 5, 3, cells, slots), f32),
            pltpu.VMEM((2 * MODES, cells * slots), bf16),
        ],
        4_000_000,
        slot_state,
    )

    def swap(message, chip_bit, column_bit):
        pairs = [
            (i * ty_size + q, ((i // 2 ^ chip_bit) * 2 + (i + 1) % 2) * ty_size + (q ^ column_bit))
            for i in range(tx_size)
            for q in range(ty_size)
        ]
        return lax.ppermute(message, ("tx", "ty"), pairs)

    def near_call(body, flops, *args):
        return call(body, near_shape, turned, flops, *args)[0]

    whole = [(r, c) for c in range(cols) for r in range(rows)]
    third = len(whole) // 4
    partner = swap(own, 0, 0)
    near_a = near_call(
        functools.partial(near_local_kernel, rows, cols, whole[:third]), 4_000_000, own
    )
    total = own[0:4] + partner[0:4]
    first = jnp.where(core == 0, own[4:7], partner[4:7])
    second = jnp.where(core == 0, partner[4:7], own[4:7])
    items = [jnp.concatenate([first[:, 0:cols], second[:, cells - cols : cells]], axis=1)]
    bit = 1
    while bit < chips:
        message = jnp.concatenate([total, items[-1]], axis=0)
        steps = (1, 2, 3) if 4 * bit <= chips else (1,)
        for step in steps:
            got = swap(message, step * bit, 0)
            total = total + got[0:4]
            if step != 2:
                items.append(got[4:7])
        bit *= len(steps) + 1
    near_b = near_call(
        functools.partial(near_local_kernel, rows, cols, whole[third : 3 * third]), 9_000_000, own
    )
    near_c = near_call(
        functools.partial(near_partner_kernel, rows, cols, whole[3 * third :]), 9_000_000,
        own, partner,
    )
    slot_of = lax.broadcasted_iota(jnp.int32, (3, 2 * cols, slots), 1)
    below = slot_of < cols
    distant = far_item(items, chip) if chips > 2 else items[1]
    ring = jnp.where(below == (chip % 2 == 0), items[1], distant)
    shift = jnp.where(below, 2.0 * rows * unit, -2.0 * rows * unit)
    which = lax.broadcasted_iota(jnp.int32, (3, 2 * cols, slots), 0)
    ring = ring + jnp.where(which == 1, shift, 0.0)
    packed, ring = call(
        functools.partial(pack_kernel, rows, cols),
        [((10, cells, slots), f32), ((3, 2 * cols, slots), f32)], [], 100_000,
        own, partner, jnp.concatenate([total, ring], axis=0),
    )
    got = swap(packed, 0, 1)
    near_d = near_call(functools.partial(near_ring_kernel, rows, cols), 5_000_000, own, ring)
    total = packed[0:4] + got[0:4]
    close = jnp.where(ty % 2 == 0, got[4:7], got[7:10])
    items = [None, jnp.where(ty % 2 == 0, got[7:10], got[4:7])]
    bit = 2
    while bit < ty_size:
        message = jnp.concatenate([total, items[-1]], axis=0)
        got = swap(message, 0, bit)
        total = total + got[0:4]
        items.append(got[4:7])
        bit *= 2
    near_e, weights, spread = call(
        functools.partial(near_close_kernel, rows, cols, cell_count),
        near_shape + [((2, HALF, 2 * MODES), f32), ((2 * rows, slots, slots), f32)],
        turned, 3_000_000,
        own, close,
    )
    distant = far_item(items, ty) if ty_size > 2 else items[1]
    last = jnp.concatenate([total, distant], axis=0)
    return tuple(
        call(
            functools.partial(final_kernel, rows, cols),
            [(offsets.shape, f32)] * 2,
            [pltpu.VMEM((2, cells, slots), f32), pltpu.VMEM((2, cells, slots), f32)],
            4_000_000,
            kept, own, x_table, y_table, last,
            near_a, near_b, near_c, near_d, near_e, weights, spread,
        )
    )


def solution(mesh):
    placed = (P(None, "tx", "ty", None), P("tx", "ty", None), P("tx", "ty"))

    return jax.shard_map(
        per_device,
        mesh=mesh,
        in_specs=placed,
        out_specs=(P(None, "tx", "ty", None), P(None, "tx", "ty", None)),
        check_vma=False,
    )
```

```python
import functools
import math

import jax
import jax.numpy as jnp
from jax import lax
from jax.experimental import pallas as pl
from jax.experimental.pallas import tpu as pltpu
from jax.sharding import PartitionSpec as P


MODES = 64
HALF = MODES // 2

two_pi = 2.0 * math.pi
screen = 1.5625
smooth = 0.0625
section_step = 0.25
unit = math.sqrt(screen / math.log(2.0))
floor_term = smooth * unit * unit

VMEM = pl.BlockSpec(memory_space=pltpu.VMEM)
PARAMS = pltpu.CompilerParams(vmem_limit_bytes=8 * 1024 * 1024)


def position():
    tx = lax.axis_index("tx")
    return tx, lax.axis_index("ty"), lax.rem(tx, 2)


def call(body, out_shapes, scratch, flops, *args):
    outs = [jax.ShapeDtypeStruct(s, d) for s, d in out_shapes]
    return pl.pallas_call(
        body,
        out_shape=outs,
        in_specs=[VMEM] * len(args),
        out_specs=[VMEM] * len(outs),
        scratch_shapes=scratch,
        compiler_params=PARAMS,
        cost_estimate=pl.CostEstimate(flops=flops, bytes_accessed=65536, transcendentals=0),
    )(*args)


def unit_circle(turn):
    quarter = jnp.floor(4.0 * turn + 0.5)
    angle = two_pi * (turn - 0.25 * quarter)
    sq = angle * angle
    sine = angle * (
        1.0 + sq * (-1.0 / 6 + sq * (1.0 / 120 + sq * (-1.0 / 5040 + sq * (1.0 / 362880))))
    )
    cosine = 1.0 + sq * (
        -0.5 + sq * (1.0 / 24 + sq * (-1.0 / 720 + sq * (1.0 / 40320 + sq * (-1.0 / 3628800))))
    )
    odd = (quarter == 1.0) | (quarter == 3.0)
    cos_neg = (quarter == 1.0) | (quarter == 2.0)
    sin_neg = (quarter == 2.0) | (quarter == 3.0)
    cos_part = jnp.where(odd, sine, cosine)
    sin_part = jnp.where(odd, cosine, sine)
    return jnp.where(cos_neg, -cos_part, cos_part), jnp.where(sin_neg, -sin_part, sin_part)


def times(p, q):
    return p[0] * q[0] - p[1] * q[1], p[0] * q[1] + p[1] * q[0]


def split(value):
    high = value.astype(jnp.bfloat16)
    low = (value - high.astype(jnp.float32)).astype(jnp.bfloat16)
    return high, low


def moments_kernel(
    rows, cols, cell_count, corner, offsets, counts, circ, own, kept, x_table, y_table, powers, weighted
):
    cells = rows * cols
    slots = circ.shape[2]
    shape = (cells, slots)
    place = position()
    cell = lax.broadcasted_iota(jnp.int32, shape, 0)
    row_in = jnp.zeros(shape, jnp.int32)
    for r in range(1, rows):
        row_in = jnp.where(cell >= r * cols, r, row_in)
    col_in = cell - row_in * cols
    slot = lax.broadcasted_iota(jnp.int32, (1, slots), 1)
    for r in range(rows):
        cells_of = pl.ds(r * cols, cols)
        kept[0, cells_of, :] = offsets[0, r]
        kept[1, cells_of, :] = offsets[1, r]
        for c in range(cols):
            count = jnp.broadcast_to(counts[pl.ds(r, 1), pl.ds(c, 1)], (1, slots))
            kept[3, pl.ds(r * cols + c, 1), :] = jnp.where(slot < count, 1.0, 0.0)
        kept[2, cells_of, :] = jnp.where(kept[3, cells_of, :] > 0.5, circ[r], 0.0)
    off_x, off_y, strength = kept[0], kept[1], kept[2]
    x_turn = ((corner[pl.ds(0, 1), :] + col_in.astype(jnp.float32)) + off_x) / cell_count
    y_turn = ((corner[pl.ds(1, 1), :] + row_in.astype(jnp.float32)) + off_y) / cell_count
    own[4] = unit * (col_in.astype(jnp.float32) + off_x)
    own[5] = unit * ((place[2] * rows + row_in).astype(jnp.float32) + off_y)
    own[6] = strength * (unit * cell_count / two_pi)
    for axis, turn in ((0, x_turn), (1, y_turn)):
        point = unit_circle(turn)
        for power in range(5):
            powers[axis, power, 0] = point[0]
            powers[axis, power, 1] = point[1]
            if power < 4:
                point = times(point, point)
    powers[0, 0, 2] = strength
    mode = lax.broadcasted_iota(jnp.int32, (8, slots), 0)
    bits = [(mode & (1 << b)) != 0 for b in range(3)]
    for i in range(cells):
        lanes = pl.ds(i * slots, slots)
        amount = jnp.broadcast_to(powers[0, 0, 2, pl.ds(i, 1), :], (8, slots))
        for axis in range(2):

            def row(power, part):
                return jnp.broadcast_to(powers[axis, power, part, pl.ds(i, 1), :], (8, slots))

            group = None
            for b in range(3):
                factor = (jnp.where(bits[b], row(b, 0), 1.0), jnp.where(bits[b], row(b, 1), 0.0))
                group = factor if group is None else times(group, factor)
            eight = (row(3, 0), row(3, 1))
            sixteen = (row(4, 0), row(4, 1))
            second = times(group, eight)
            groups = [group, second, times(group, sixteen), times(second, sixteen)]
            wave = jnp.concatenate([g[0] for g in groups] + [g[1] for g in groups], axis=0)
            if axis == 0:
                x_table[:, lanes] = wave
                high, low = split(wave * jnp.concatenate([amount] * 8, axis=0))
                weighted[0:MODES, lanes] = high
                weighted[MODES : 2 * MODES, lanes] = low
            else:
                high, low = split(wave)
                y_table[0:MODES, lanes] = high
                y_table[MODES : 2 * MODES, lanes] = low
    full = lax.dot_general(
        weighted[...],
        y_table[...],
        (((1,), (1,)), ((), ())),
        preferred_element_type=jnp.float32,
    )
    full = full[0:MODES] + full[MODES : 2 * MODES]
    full = full + pltpu.roll(full, MODES, 1)
    lane = lax.broadcasted_iota(jnp.int32, (HALF, 2 * MODES), 1)
    own[0:4] = jnp.where(lane < MODES, full[0:HALF], full[HALF:MODES]).reshape(4, 8, 2 * MODES)


def pair_terms(target, source, total):
    offset_x = target[0] - source[0]
    offset_y = target[1] - source[1]
    square = offset_x * offset_x + offset_y * offset_y
    weight = source[2] / ((square + floor_term) * jnp.exp2(square))
    return total[0] - offset_y * weight, total[1] + offset_x * weight


def near_sum(sources, targets, links, turned, most=48):
    slots = sources[0][0].shape[1]
    stack = [part for source in sources for part in source]
    pad = -len(stack) % 8
    stack = jnp.concatenate(stack + [jnp.zeros((pad, slots), jnp.float32)] * (pad > 0), axis=0)
    turned[:, 0 : stack.shape[0]] = stack.T
    spread = [tuple(jnp.broadcast_to(part, (8, slots)) for part in t) for t in targets]

    def step(k, totals):
        totals = list(totals)
        chunk = turned[pl.ds(8 * k if isinstance(k, int) else pl.multiple_of(8 * k, 8), 8), :]
        for i, reached in enumerate(links):
            source = tuple(
                jnp.broadcast_to(chunk[:, 3 * i + part : 3 * i + part + 1], (8, slots))
                for part in range(3)
            )
            for t in reached:
                totals[2 * t], totals[2 * t + 1] = pair_terms(
                    spread[t], source, (totals[2 * t], totals[2 * t + 1])
                )
        return tuple(totals)

    zero = jnp.zeros((8, slots), jnp.float32)
    pairs = sum(len(reached) for reached in links)
    chunks = slots // 8
    group = 1
    while group * 2 * pairs <= most and chunks % (group * 2) == 0:
        group *= 2

    def grouped(k, totals):
        for u in range(group):
            totals = step(k * group + u, totals)
        return totals

    totals = (zero,) * (2 * len(targets))
    if group == chunks:
        totals = grouped(0, totals)
    else:
        totals = lax.fori_loop(0, chunks // group, grouped, totals)
    return [jnp.sum(total, axis=0, keepdims=True) for total in totals]


def reach(col, cols):
    return [c for c in (col - 1, col, col + 1) if 0 <= c < cols]


def read_row(ref, base, at):
    return tuple(ref[base + part, pl.ds(at, 1), :] for part in range(3))


def near_last_cols(rows, cols, side, spread, right, near):
    slots = side.shape[2]
    shift = jnp.where(right == 1, unit * cols, -unit * cols)
    sources = []
    for k in range(rows + 2):
        row = (
            side[4, pl.ds(k, 1), :] + shift,
            side[4, pl.ds(rows + 2 + k, 1), :],
            side[5, pl.ds(k, 1), :],
        )
        sources.append(tuple(jnp.broadcast_to(part, (8, slots)) for part in row))
    stack = []
    for r in range(rows):
        parts = ([], [])
        for k in range(slots // 8):
            target = tuple(spread[2 * r + part, 8 * k : 8 * k + 8] for part in range(2))
            total = (0.0, 0.0)
            for i in range(r, r + 3):
                total = pair_terms(target, sources[i], total)
            parts[0].append(total[0])
            parts[1].append(total[1])
        stack += parts[0] + parts[1]
    high, low = split(jnp.concatenate(stack, axis=0))
    ones = jnp.ones((8, slots), jnp.bfloat16)

    def lanes_sum(value):
        return lax.dot_general(
            ones, value, (((1,), (1,)), ((), ())), preferred_element_type=jnp.float32
        )

    sums = lanes_sum(high) + lanes_sum(low)
    edge = jnp.where(right == 1, cols - 1, 0)
    for r in range(rows):
        for part in range(2):
            at = pl.ds(r * cols + edge, 1)
            lanes = slice((2 * r + part) * slots, (2 * r + part + 1) * slots)
            near[part, at, :] = near[part, at, :] + sums[0:1, lanes]


def near_local(rows, cols, own, cells, near, turned):
    places = sorted({(r, c) for row, col in cells for r in range(rows) if abs(r - row) <= 1 for c in reach(col, cols)})
    sources = [read_row(own, 4, r * cols + c) for r, c in cells]
    targets = [read_row(own, 4, r * cols + c)[:2] for r, c in places]
    links = [
        [t for t, (r, c) in enumerate(places) if abs(r - row) <= 1 and abs(c - col) <= 1]
        for row, col in cells
    ]
    sums = near_sum(sources, targets, links, turned)
    for t, (r, c) in enumerate(places):
        for part in range(2):
            at = pl.ds(r * cols + c, 1)
            near[part, at, :] = near[part, at, :] + sums[2 * t + part]


def near_local_kernel(rows, cols, cells, own, near, turned):
    near[...] = jnp.zeros_like(near)
    near_local(rows, cols, own, cells, near, turned)


def near_rows(rows, cols, own, outer, base, above, near, turned):
    def pick(ref, origin, part, first, second):
        return jnp.where(
            above == 1, ref[origin + part, pl.ds(first, 1), :], ref[origin + part, pl.ds(second, 1), :]
        )

    sources = [
        tuple(pick(outer, base, part, cols + c, c) for part in range(3)) for c in range(cols)
    ]
    last = (rows - 1) * cols
    targets = [tuple(pick(own, 4, part, c, last + c) for part in range(2)) for c in range(cols)]
    sums = near_sum(sources, targets, [reach(c, cols) for c in range(cols)], turned)
    top = jnp.where(above == 1, 0, last)
    for c in range(cols):
        for part in range(2):
            at = pl.ds(top + c, 1)
            near[part, at, :] = near[part, at, :] + sums[2 * c + part]


def near_cols(rows, cols, own, side, base, right, near, turned, most=48):
    shift = jnp.where(right == 1, unit * cols, -unit * cols)
    sources = []
    for k in range(rows + 2):
        row = read_row(side, base, k)
        sources.append((row[0] + shift, row[1], row[2]))
    edge = jnp.where(right == 1, cols - 1, 0)
    targets = [read_row(own, 4, r * cols + edge)[:2] for r in range(rows)]
    links = [[r for r in range(rows) if 0 <= k - r <= 2] for k in range(rows + 2)]
    sums = near_sum(sources, targets, links, turned, most)
    for r in range(rows):
        for part in range(2):
            at = pl.ds(r * cols + edge, 1)
            near[part, at, :] = near[part, at, :] + sums[2 * r + part]


def near_partner_kernel(rows, cols, cells, own, partner, near, turned):
    place = position()
    near[...] = jnp.zeros_like(near)
    near_local(rows, cols, own, cells, near, turned)
    near_rows(rows, cols, own, partner, 4, place[2], near, turned)


def near_ring_kernel(rows, cols, own, ring, near, turned):
    place = position()
    near[...] = jnp.zeros_like(near)
    near_rows(rows, cols, own, ring, 0, 1 - place[2], near, turned)


def near_close_kernel(rows, cols, cell_count, own, close, near, weights, spread, turned):
    shape = (HALF, 2 * MODES)
    lane = lax.broadcasted_iota(jnp.int32, shape, 1)
    m = lax.broadcasted_iota(jnp.int32, shape, 0).astype(jnp.float32)
    n = (lane & (HALF - 1)).astype(jnp.float32)
    square = (two_pi * two_pi) * (m * m + n * n)
    keep = square > 0.0
    safe = jnp.where(keep, square, 1.0)
    damping = jnp.where(keep, jnp.exp(-safe / (6.25 * cell_count * cell_count)) / safe, 0.0)
    damping = damping * (4.0 * two_pi)
    u_weight = damping * n * jnp.where(m == 0.0, 0.5, 1.0)
    v_weight = damping * m * jnp.where(n == 0.0, 0.5, 1.0)
    weights[0] = u_weight
    weights[1] = v_weight
    place = position()
    near[...] = jnp.zeros_like(near)
    right = 1 - lax.rem(place[1], 2)
    slots = own.shape[2]
    edge = jnp.where(right == 1, 0, cols - 1)
    for r in range(rows):
        for part in range(2):
            row = own[4 + part, pl.ds(r * cols + edge, 1), :]
            spread[2 * r + part] = jnp.broadcast_to(row, (slots, slots)).T
    near_cols(rows, cols, own, close, 0, right, near, turned)


def put_row(message, parts):
    message[4] = jnp.concatenate(parts[0:2], axis=0)
    message[5] = jnp.concatenate([parts[2], jnp.zeros_like(parts[2])], axis=0)


def get_row(message, cols):
    return message[4, 0:cols], message[4, cols : 2 * cols], message[5, 0:cols]


def chip_even():
    return lax.rem(lax.div(lax.axis_index("tx"), 2), 2) == 0


def join_kernel(rows, cols, own, partner, message, across, corner):
    core = position()[2]
    last = (rows - 1) * cols
    total = own[0:4] + partner[0:4]
    for target in (message, across, corner):
        target[0:4] = total
    even = chip_even()
    near_parts, far_parts = [], []
    for at in range(4, 7):
        first_row = jnp.where(core == 0, own[at, 0:cols], partner[at, 0:cols])
        last_row = jnp.where(core == 0, partner[at, last:], own[at, last:])
        near_parts.append(jnp.where(even, last_row, first_row))
        far_parts.append(jnp.where(even, first_row, last_row))
    put_row(message, near_parts)
    put_row(corner, far_parts)


def pack_kernel(rows, cols, own, partner, message, near_item, far_item, *others):
    got, (packed, ring) = others[:-2], others[-2:]
    core = position()[2]
    even = chip_even()
    total = message[0:4]
    for item in got:
        total = total + item[0:4]
    packed[0:4] = total
    shift = 2.0 * rows * unit
    for part, (close, distant) in enumerate(zip(get_row(near_item, cols), get_row(far_item, cols))):
        below = jnp.where(even, close, distant)
        above = jnp.where(even, distant, close)
        if part == 1:
            below, above = below + shift, above - shift
        ring[part] = jnp.concatenate([below, above], axis=0)
    near_col = jnp.where(lax.rem(lax.axis_index("ty"), 2) == 0, cols - 1, 0)
    for part in range(3):
        own_of, partner_of = own.at[4 + part], partner.at[4 + part]
        for base, col in ((0, near_col), (rows + 2, cols - 1 - near_col)):

            def cell(ref, r):
                return ref[pl.ds(r * cols + col, 1), :]

            over = ring[part, pl.ds(cols + col, 1), :]
            under = ring[part, pl.ds(col, 1), :]
            mine = [cell(own_of, r) for r in range(rows)]
            other = [cell(partner_of, r) for r in range(rows)]
            if base == 0:
                entries = (
                    [jnp.where(core == 0, mine[-1], over)]
                    + other
                    + [jnp.where(core == 0, under, mine[0])]
                )
            else:
                entries = (
                    [jnp.where(core == 0, over, other[-1])]
                    + mine
                    + [jnp.where(core == 0, other[0], under)]
                )
            for k, entry in enumerate(entries):
                packed[4 + part, pl.ds(base + k, 1), :] = entry


def turn_kernel(rows, packed, got, message, close):
    count = rows + 2
    message[0:4] = packed[0:4] + got[0:4]
    put_row(message, [got[4 + part, count : 2 * count] for part in range(3)])
    for part in range(3):
        close[part, 0:count] = got[4 + part, 0:count]


def final_kernel(
    rows, cols, kept, own, x_table, y_table, message, got, last,
    near_a, near_b, near_c, near_d, near_e, weights, spread, velocity, moved, near, far,
):
    cells = rows * cols
    slots = own.shape[2]
    place = position()
    shape = (HALF, 2 * MODES)
    lane = lax.broadcasted_iota(jnp.int32, shape, 1)
    total = (message[0:4] + got[0:4]).reshape(shape)
    y_odd = (lane & HALF) != 0
    swapped = jnp.where(y_odd, -pltpu.roll(total, HALF, 1), pltpu.roll(total, 2 * MODES - HALF, 1))
    u_part = weights[0] * swapped
    crossed = pltpu.roll(total, MODES, 1)
    v_part = weights[1] * jnp.where(lane < MODES, -crossed, crossed)
    left = []
    for part in (u_part, v_part):
        other = pltpu.roll(part, MODES, 1)
        for doubled in (
            jnp.where(lane < MODES, part, other),
            jnp.where(lane < MODES, other, part),
        ):
            left.append(jnp.concatenate(split(doubled), axis=1))
    left = jnp.concatenate(left, axis=0)
    right = jnp.concatenate([y_table[...], y_table[...]], axis=0)
    terms = jnp.dot(left, right, preferred_element_type=jnp.float32)
    for i in range(cells):
        lanes = slice(i * slots, (i + 1) * slots)
        wave = x_table[:, lanes]
        far[0, pl.ds(i, 1), :] = jnp.sum(terms[0:MODES, lanes] * wave, axis=0, keepdims=True)
        far[1, pl.ds(i, 1), :] = jnp.sum(terms[MODES:, lanes] * wave, axis=0, keepdims=True)
    near[...] = (near_a[...] + near_b[...]) + (near_c[...] + near_d[...]) + near_e[...]
    near_last_cols(rows, cols, last, spread, lax.rem(place[1], 2), near)
    live = kept[3] > 0.5
    for part in range(2):
        value = jnp.where(live, near[part] + far[part], 0.0)
        after = kept[part] + section_step * value
        for r in range(rows):
            velocity[part, r] = value[r * cols : (r + 1) * cols]
            moved[part, r] = after[r * cols : (r + 1) * cols]


def far_item(items, index):
    if len(items) == 3:
        return items[2]
    count = 1 << (len(items) - 1)
    up = jnp.where(index % 2 == 1, (index + 1) % count, (index + count - 1) % count)
    mask = index ^ up
    chosen = items[-1]
    for k in range(2, len(items) - 1):
        chosen = jnp.where(mask == (1 << k) - 1, items[k], chosen)
    return chosen


def per_device(offsets, circ, counts):
    rows, cols, slots = circ.shape
    cells = rows * cols
    tx_size, ty_size = lax.axis_size("tx"), lax.axis_size("ty")
    chips = tx_size // 2
    cell_count = rows * tx_size
    tx, ty = lax.axis_index("tx"), lax.axis_index("ty")
    chip = tx // 2
    f32, bf16 = jnp.float32, jnp.bfloat16
    turned = [pltpu.VMEM((slots, 128), f32)]
    near_shape = [((2, cells, slots), f32)]

    first_cell = jnp.stack([ty * cols, tx * rows, tx]).astype(jnp.int32)
    corner = jnp.broadcast_to(first_cell[:, None], (3, slots)).astype(f32)
    own, kept, x_table, y_table = call(
        functools.partial(moments_kernel, rows, cols, cell_count),
        [
            ((7, cells, slots), f32),
            ((4, cells, slots), f32),
            ((MODES, cells * slots), f32),
            ((2 * MODES, cells * slots), bf16),
        ],
        [
            pltpu.VMEM((2, 5, 3, cells, slots), f32),
            pltpu.VMEM((2 * MODES, cells * slots), bf16),
        ],
        4_000_000,
        corner, offsets, counts, circ,
    )

    def swap(message, chip_bit, column_bit, flip=True):
        pairs = [
            (i * ty_size + q, ((i // 2 ^ chip_bit) * 2 + (i + flip) % 2) * ty_size + (q ^ column_bit))
            for i in range(tx_size)
            for q in range(ty_size)
        ]
        return lax.ppermute(message, ("tx", "ty"), pairs)

    def near_call(body, flops, *args):
        return call(body, near_shape, turned, flops, *args)[0]

    whole = [(r, c) for c in range(cols) for r in range(rows)]
    third = len(whole) // 4
    partner = swap(own, 0, 0)
    near_a = near_call(
        functools.partial(near_local_kernel, rows, cols, whole[:third]), 4_000_000, own
    )
    tile = (cells, slots)
    six = ((6,) + tile, f32)
    first, across, corner = call(
        functools.partial(join_kernel, rows, cols), [six, ((4,) + tile, f32), six], [], 50_000,
        own, partner,
    )
    message = first
    items = [message]
    bit = 1
    while True:
        if bit == 1:
            sent = (first, across, corner)
        else:
            sent = (message,) * 3
        steps = (1, 2, 3) if 4 * bit <= chips else (1,)
        arrived = [swap(part, step * bit, 0, bit == 1) for step, part in zip(steps, sent)]
        items += arrived[::2]
        bit *= len(steps) + 1
        if bit >= chips:
            break
        message = jnp.concatenate([message[0:4] + sum(got[0:4] for got in arrived), items[-1][4:6]])
    near_b = near_call(
        functools.partial(near_local_kernel, rows, cols, whole[third : 3 * third]), 9_000_000, own
    )
    near_c = near_call(
        functools.partial(near_partner_kernel, rows, cols, whole[3 * third :]), 9_000_000,
        own, partner,
    )
    packed, ring = call(
        functools.partial(pack_kernel, rows, cols),
        [((7,) + tile, f32), ((3,) + tile, f32)], [], 100_000,
        own, partner, message, items[1], far_item(items, chip), *arrived,
    )
    got = swap(packed, 0, 1)
    near_d = near_call(functools.partial(near_ring_kernel, rows, cols), 5_000_000, own, ring)
    message, close = call(
        functools.partial(turn_kernel, rows), [six, ((3, rows + 2, slots), f32)], [], 50_000,
        packed, got,
    )
    items = [None, message]
    bit = 2
    while True:
        got = swap(message, 0, bit, bit == 2)
        items.append(got)
        bit *= 2
        if bit >= ty_size:
            break
        message = jnp.concatenate([message[0:4] + got[0:4], got[4:6]])
    near_e, weights, spread = call(
        functools.partial(near_close_kernel, rows, cols, cell_count),
        near_shape + [((2, HALF, 2 * MODES), f32), ((2 * rows, slots, slots), f32)],
        turned, 3_000_000,
        own, close,
    )
    return tuple(
        call(
            functools.partial(final_kernel, rows, cols),
            [(offsets.shape, f32)] * 2,
            [pltpu.VMEM((2, cells, slots), f32), pltpu.VMEM((2, cells, slots), f32)],
            4_000_000,
            kept, own, x_table, y_table, message, got, far_item(items, ty),
            near_a, near_b, near_c, near_d, near_e, weights, spread,
        )
    )


def solution(mesh):
    placed = (P(None, "tx", "ty", None), P("tx", "ty", None), P("tx", "ty"))

    return jax.shard_map(
        per_device,
        mesh=mesh,
        in_specs=placed,
        out_specs=(P(None, "tx", "ty", None), P(None, "tx", "ty", None)),
        check_vma=False,
    )
```

```python
import functools
import math

import jax
import jax.numpy as jnp
from jax import lax
from jax.experimental import pallas as pl
from jax.experimental.pallas import tpu as pltpu
from jax.sharding import PartitionSpec as P


MODES = 64
HALF = MODES // 2

two_pi = 2.0 * math.pi
screen = 1.5625
smooth = 0.0625
section_step = 0.25
unit = math.sqrt(screen / math.log(2.0))
floor_term = smooth * unit * unit

VMEM = pl.BlockSpec(memory_space=pltpu.VMEM)
PARAMS = pltpu.CompilerParams(vmem_limit_bytes=8 * 1024 * 1024)


def position():
    tx = lax.axis_index("tx")
    return tx, lax.axis_index("ty"), lax.rem(tx, 2)


def call(body, out_shapes, scratch, flops, *args):
    outs = [jax.ShapeDtypeStruct(s, d) for s, d in out_shapes]
    return pl.pallas_call(
        body,
        out_shape=outs,
        in_specs=[VMEM] * len(args),
        out_specs=[VMEM] * len(outs),
        scratch_shapes=scratch,
        compiler_params=PARAMS,
        cost_estimate=pl.CostEstimate(flops=flops, bytes_accessed=65536, transcendentals=0),
    )(*args)


def unit_circle(turn):
    quarter = jnp.floor(4.0 * turn + 0.5)
    angle = two_pi * (turn - 0.25 * quarter)
    sq = angle * angle
    sine = angle * (
        1.0 + sq * (-1.0 / 6 + sq * (1.0 / 120 + sq * (-1.0 / 5040 + sq * (1.0 / 362880))))
    )
    cosine = 1.0 + sq * (
        -0.5 + sq * (1.0 / 24 + sq * (-1.0 / 720 + sq * (1.0 / 40320 + sq * (-1.0 / 3628800))))
    )
    odd = (quarter == 1.0) | (quarter == 3.0)
    cos_neg = (quarter == 1.0) | (quarter == 2.0)
    sin_neg = (quarter == 2.0) | (quarter == 3.0)
    cos_part = jnp.where(odd, sine, cosine)
    sin_part = jnp.where(odd, cosine, sine)
    return jnp.where(cos_neg, -cos_part, cos_part), jnp.where(sin_neg, -sin_part, sin_part)


def times(p, q):
    return p[0] * q[0] - p[1] * q[1], p[0] * q[1] + p[1] * q[0]


def split(value):
    high = value.astype(jnp.bfloat16)
    low = (value - high.astype(jnp.float32)).astype(jnp.bfloat16)
    return high, low


def moments_kernel(
    rows, cols, cell_count, corner, offsets, counts, circ, own, kept, x_table, y_table,
    powers, amounts,
):
    cells = rows * cols
    slots = circ.shape[2]
    shape = (cells, slots)
    place = position()
    cell = lax.broadcasted_iota(jnp.int32, shape, 0)
    row_in = jnp.zeros(shape, jnp.int32)
    for r in range(1, rows):
        row_in = jnp.where(cell >= r * cols, r, row_in)
    col_in = cell - row_in * cols
    slot = lax.broadcasted_iota(jnp.int32, (1, slots), 1)
    for r in range(rows):
        cells_of = pl.ds(r * cols, cols)
        kept[0, cells_of, :] = offsets[0, r]
        kept[1, cells_of, :] = offsets[1, r]
        for c in range(cols):
            count = jnp.broadcast_to(counts[pl.ds(r, 1), pl.ds(c, 1)], (1, slots))
            kept[3, pl.ds(r * cols + c, 1), :] = jnp.where(slot < count, 1.0, 0.0)
        kept[2, cells_of, :] = jnp.where(kept[3, cells_of, :] > 0.5, circ[r], 0.0)
    off_x, off_y, strength = kept[0], kept[1], kept[2]
    x_turn = ((corner[pl.ds(0, 1), :] + col_in.astype(jnp.float32)) + off_x) / cell_count
    y_turn = ((corner[pl.ds(1, 1), :] + row_in.astype(jnp.float32)) + off_y) / cell_count
    own[4] = unit * (col_in.astype(jnp.float32) + off_x)
    own[5] = unit * ((place[2] * rows + row_in).astype(jnp.float32) + off_y)
    own[6] = strength * (unit * cell_count / two_pi)
    amounts[...] = strength
    for axis, turn in ((0, x_turn), (1, y_turn)):
        one = unit_circle(turn)
        two = times(one, one)
        three = times(two, one)
        four = times(two, two)
        low_modes = [
            (jnp.ones(shape, jnp.float32), jnp.zeros(shape, jnp.float32)),
            one, two, three, four, times(four, one), times(four, two), times(four, three),
        ]
        eight = times(four, four)
        for k, point in enumerate(low_modes + [eight, times(eight, eight)]):
            for part in range(2):
                powers[axis, part, k * cells : (k + 1) * cells] = point[part]
    full = None
    pair = 2 if cells % 2 == 0 else 1
    for i in range(0, cells, pair):
        left, right = [], []
        for cell_at in range(i, i + pair):
            lanes = pl.ds(cell_at * slots, slots)
            amount = jnp.broadcast_to(amounts[pl.ds(cell_at, 1), :], (8, slots))
            for axis, table, parts in ((0, x_table, left), (1, y_table, right)):

                def row(k, part):
                    at = pl.ds(k * cells + cell_at, 1)
                    return jnp.broadcast_to(powers[axis, part, at, :], (8, slots))

                group = tuple(
                    powers[axis, part, pl.ds(cell_at, 8, stride=cells), :] for part in range(2)
                )
                second = times(group, (row(8, 0), row(8, 1)))
                sixteen = (row(9, 0), row(9, 1))
                groups = [group, second, times(group, sixteen), times(second, sixteen)]
                wave = [g[0] for g in groups] + [g[1] for g in groups]
                table[:, lanes] = jnp.concatenate(wave, axis=0)
                if axis == 0:
                    wave = [piece * amount for piece in wave]
                parts.append(jnp.concatenate(split(jnp.concatenate(wave, axis=0)), axis=0))
        product = lax.dot_general(
            jnp.concatenate(left, axis=1),
            jnp.concatenate(right, axis=1),
            (((1,), (1,)), ((), ())),
            preferred_element_type=jnp.float32,
        )
        full = product if full is None else full + product
    full = full[0:MODES] + full[MODES : 2 * MODES]
    full = full + pltpu.roll(full, MODES, 1)
    lane = lax.broadcasted_iota(jnp.int32, (HALF, 2 * MODES), 1)
    own[0:4] = jnp.where(lane < MODES, full[0:HALF], full[HALF:MODES]).reshape(4, 8, 2 * MODES)


def pair_terms(target, source, total):
    offset_x = target[0] - source[0]
    offset_y = target[1] - source[1]
    square = offset_x * offset_x + offset_y * offset_y
    weight = source[2] / ((square + floor_term) * jnp.exp2(square))
    return total[0] - offset_y * weight, total[1] + offset_x * weight


def near_sum(sources, targets, links, turned, most=48):
    slots = sources[0][0].shape[1]
    stack = [part for source in sources for part in source]
    pad = -len(stack) % 8
    stack = jnp.concatenate(stack + [jnp.zeros((pad, slots), jnp.float32)] * (pad > 0), axis=0)
    turned[:, 0 : stack.shape[0]] = stack.T
    spread = [tuple(jnp.broadcast_to(part, (8, slots)) for part in t) for t in targets]

    def step(k, totals):
        totals = list(totals)
        chunk = turned[pl.ds(8 * k if isinstance(k, int) else pl.multiple_of(8 * k, 8), 8), :]
        for i, reached in enumerate(links):
            source = tuple(
                jnp.broadcast_to(chunk[:, 3 * i + part : 3 * i + part + 1], (8, slots))
                for part in range(3)
            )
            for t in reached:
                totals[2 * t], totals[2 * t + 1] = pair_terms(
                    spread[t], source, (totals[2 * t], totals[2 * t + 1])
                )
        return tuple(totals)

    zero = jnp.zeros((8, slots), jnp.float32)
    pairs = sum(len(reached) for reached in links)
    chunks = slots // 8
    group = 1
    while group * 2 * pairs <= most and chunks % (group * 2) == 0:
        group *= 2

    def grouped(k, totals):
        for u in range(group):
            totals = step(k * group + u, totals)
        return totals

    totals = (zero,) * (2 * len(targets))
    if group == chunks:
        totals = grouped(0, totals)
    else:
        totals = lax.fori_loop(0, chunks // group, grouped, totals)
    return [jnp.sum(total, axis=0, keepdims=True) for total in totals]


def reach(col, cols):
    return [c for c in (col - 1, col, col + 1) if 0 <= c < cols]


def read_row(ref, base, at):
    return tuple(ref[base + part, pl.ds(at, 1), :] for part in range(3))


def near_last_cols(rows, cols, side, spread, right, near):
    slots = side.shape[2]
    shift = jnp.where(right == 1, unit * cols, -unit * cols)
    sources = []
    for k in range(rows + 2):
        row = (
            side[4, pl.ds(k, 1), :] + shift,
            side[4, pl.ds(rows + 2 + k, 1), :],
            side[5, pl.ds(k, 1), :],
        )
        sources.append(tuple(jnp.broadcast_to(part, (8, slots)) for part in row))
    stack = []
    for r in range(rows):
        parts = ([], [])
        for k in range(slots // 8):
            target = tuple(spread[2 * r + part, 8 * k : 8 * k + 8] for part in range(2))
            total = (0.0, 0.0)
            for i in range(r, r + 3):
                total = pair_terms(target, sources[i], total)
            parts[0].append(total[0])
            parts[1].append(total[1])
        stack += parts[0] + parts[1]
    high, low = split(jnp.concatenate(stack, axis=0))
    ones = jnp.ones((8, slots), jnp.bfloat16)

    def lanes_sum(value):
        return lax.dot_general(
            ones, value, (((1,), (1,)), ((), ())), preferred_element_type=jnp.float32
        )

    sums = lanes_sum(high) + lanes_sum(low)
    edge = jnp.where(right == 1, cols - 1, 0)
    for r in range(rows):
        for part in range(2):
            at = pl.ds(r * cols + edge, 1)
            lanes = slice((2 * r + part) * slots, (2 * r + part + 1) * slots)
            near[part, at, :] = near[part, at, :] + sums[0:1, lanes]


def near_local(rows, cols, own, cells, near, turned):
    if not cells:
        return
    places = sorted({(r, c) for row, col in cells for r in range(rows) if abs(r - row) <= 1 for c in reach(col, cols)})
    sources = [read_row(own, 4, r * cols + c) for r, c in cells]
    targets = [read_row(own, 4, r * cols + c)[:2] for r, c in places]
    links = [
        [t for t, (r, c) in enumerate(places) if abs(r - row) <= 1 and abs(c - col) <= 1]
        for row, col in cells
    ]
    sums = near_sum(sources, targets, links, turned)
    for t, (r, c) in enumerate(places):
        for part in range(2):
            at = pl.ds(r * cols + c, 1)
            near[part, at, :] = near[part, at, :] + sums[2 * t + part]


def near_local_kernel(rows, cols, cells, own, near, turned):
    near[...] = jnp.zeros_like(near)
    near_local(rows, cols, own, cells, near, turned)


def near_rows(rows, cols, own, outer, base, above, near, turned):
    def pick(ref, origin, part, first, second):
        return jnp.where(
            above == 1, ref[origin + part, pl.ds(first, 1), :], ref[origin + part, pl.ds(second, 1), :]
        )

    sources = [
        tuple(pick(outer, base, part, cols + c, c) for part in range(3)) for c in range(cols)
    ]
    last = (rows - 1) * cols
    targets = [tuple(pick(own, 4, part, c, last + c) for part in range(2)) for c in range(cols)]
    sums = near_sum(sources, targets, [reach(c, cols) for c in range(cols)], turned)
    top = jnp.where(above == 1, 0, last)
    for c in range(cols):
        for part in range(2):
            at = pl.ds(top + c, 1)
            near[part, at, :] = near[part, at, :] + sums[2 * c + part]


def near_cols(rows, cols, own, side, base, right, near, turned, most=48):
    shift = jnp.where(right == 1, unit * cols, -unit * cols)
    sources = []
    for k in range(rows + 2):
        row = read_row(side, base, k)
        sources.append((row[0] + shift, row[1], row[2]))
    edge = jnp.where(right == 1, cols - 1, 0)
    targets = [read_row(own, 4, r * cols + edge)[:2] for r in range(rows)]
    links = [[r for r in range(rows) if 0 <= k - r <= 2] for k in range(rows + 2)]
    sums = near_sum(sources, targets, links, turned, most)
    for r in range(rows):
        for part in range(2):
            at = pl.ds(r * cols + edge, 1)
            near[part, at, :] = near[part, at, :] + sums[2 * r + part]


def near_partner_kernel(rows, cols, cells, own, partner, near, turned):
    place = position()
    near[...] = jnp.zeros_like(near)
    near_local(rows, cols, own, cells, near, turned)
    near_rows(rows, cols, own, partner, 4, place[2], near, turned)


def near_ring_kernel(rows, cols, own, ring, near, turned):
    place = position()
    near[...] = jnp.zeros_like(near)
    near_rows(rows, cols, own, ring, 0, 1 - place[2], near, turned)


def near_close_kernel(
    rows, cols, cell_count, own, close, y_wave, near, weights, spread, y_table, turned
):
    high, low = split(y_wave[...])
    y_table[0:MODES] = high
    y_table[MODES : 2 * MODES] = low
    shape = (HALF, 2 * MODES)
    lane = lax.broadcasted_iota(jnp.int32, shape, 1)
    m = lax.broadcasted_iota(jnp.int32, shape, 0).astype(jnp.float32)
    n = (lane & (HALF - 1)).astype(jnp.float32)
    square = (two_pi * two_pi) * (m * m + n * n)
    keep = square > 0.0
    safe = jnp.where(keep, square, 1.0)
    damping = jnp.where(keep, jnp.exp(-safe / (6.25 * cell_count * cell_count)) / safe, 0.0)
    damping = damping * (4.0 * two_pi)
    u_weight = damping * n * jnp.where(m == 0.0, 0.5, 1.0)
    v_weight = damping * m * jnp.where(n == 0.0, 0.5, 1.0)
    weights[0] = u_weight
    weights[1] = v_weight
    place = position()
    near[...] = jnp.zeros_like(near)
    right = 1 - lax.rem(place[1], 2)
    slots = own.shape[2]
    edge = jnp.where(right == 1, 0, cols - 1)
    for r in range(rows):
        for part in range(2):
            row = own[4 + part, pl.ds(r * cols + edge, 1), :]
            spread[2 * r + part] = jnp.broadcast_to(row, (slots, slots)).T
    near_cols(rows, cols, own, close, 0, right, near, turned)


def put_row(message, parts):
    message[4] = jnp.concatenate(parts[0:2], axis=0)
    message[5] = jnp.concatenate([parts[2], jnp.zeros_like(parts[2])], axis=0)


def get_row(message, cols):
    return message[4, 0:cols], message[4, cols : 2 * cols], message[5, 0:cols]


def chip_even():
    return lax.rem(lax.div(lax.axis_index("tx"), 2), 2) == 0


def join_kernel(rows, cols, own, partner, message, across, corner):
    core = position()[2]
    last = (rows - 1) * cols
    total = own[0:4] + partner[0:4]
    for target in (message, across, corner):
        target[0:4] = total
    even = chip_even()
    near_parts, far_parts = [], []
    for at in range(4, 7):
        first_row = jnp.where(core == 0, own[at, 0:cols], partner[at, 0:cols])
        last_row = jnp.where(core == 0, partner[at, last:], own[at, last:])
        near_parts.append(jnp.where(even, last_row, first_row))
        far_parts.append(jnp.where(even, first_row, last_row))
    put_row(message, near_parts)
    put_row(corner, far_parts)


def pack_kernel(rows, cols, own, partner, message, near_item, far_item, *others):
    got, (packed, ring) = others[:-2], others[-2:]
    core = position()[2]
    even = chip_even()
    total = message[0:4]
    for item in got:
        total = total + item[0:4]
    packed[0:4] = total
    shift = 2.0 * rows * unit
    for part, (close, distant) in enumerate(zip(get_row(near_item, cols), get_row(far_item, cols))):
        below = jnp.where(even, close, distant)
        above = jnp.where(even, distant, close)
        if part == 1:
            below, above = below + shift, above - shift
        ring[part] = jnp.concatenate([below, above], axis=0)
    near_col = jnp.where(lax.rem(lax.axis_index("ty"), 2) == 0, cols - 1, 0)
    for part in range(3):
        own_of, partner_of = own.at[4 + part], partner.at[4 + part]
        for base, col in ((0, near_col), (rows + 2, cols - 1 - near_col)):

            def cell(ref, r):
                return ref[pl.ds(r * cols + col, 1), :]

            over = ring[part, pl.ds(cols + col, 1), :]
            under = ring[part, pl.ds(col, 1), :]
            mine = [cell(own_of, r) for r in range(rows)]
            other = [cell(partner_of, r) for r in range(rows)]
            if base == 0:
                entries = (
                    [jnp.where(core == 0, mine[-1], over)]
                    + other
                    + [jnp.where(core == 0, under, mine[0])]
                )
            else:
                entries = (
                    [jnp.where(core == 0, over, other[-1])]
                    + mine
                    + [jnp.where(core == 0, other[0], under)]
                )
            for k, entry in enumerate(entries):
                packed[4 + part, pl.ds(base + k, 1), :] = entry


def turn_kernel(rows, packed, got, message, close):
    count = rows + 2
    message[0:4] = packed[0:4] + got[0:4]
    put_row(message, [got[4 + part, count : 2 * count] for part in range(3)])
    for part in range(3):
        close[part, 0:count] = got[4 + part, 0:count]


def final_kernel(
    rows, cols, kept, own, x_table, y_table, message, got, last,
    near_a, near_b, near_c, near_d, near_e, weights, spread, velocity, moved, near, far,
):
    cells = rows * cols
    slots = own.shape[2]
    place = position()
    shape = (HALF, 2 * MODES)
    lane = lax.broadcasted_iota(jnp.int32, shape, 1)
    total = (message[0:4] + got[0:4]).reshape(shape)
    y_odd = (lane & HALF) != 0
    swapped = jnp.where(y_odd, -pltpu.roll(total, HALF, 1), pltpu.roll(total, 2 * MODES - HALF, 1))
    u_part = weights[0] * swapped
    crossed = pltpu.roll(total, MODES, 1)
    v_part = weights[1] * jnp.where(lane < MODES, -crossed, crossed)
    left = []
    for part in (u_part, v_part):
        other = pltpu.roll(part, MODES, 1)
        for doubled in (
            jnp.where(lane < MODES, part, other),
            jnp.where(lane < MODES, other, part),
        ):
            left.append(jnp.concatenate(split(doubled), axis=1))
    left = jnp.concatenate(left, axis=0)
    right = jnp.concatenate([y_table[...], y_table[...]], axis=0)
    terms = jnp.dot(left, right, preferred_element_type=jnp.float32)
    for i in range(cells):
        lanes = slice(i * slots, (i + 1) * slots)
        wave = x_table[:, lanes]
        far[0, pl.ds(i, 1), :] = jnp.sum(terms[0:MODES, lanes] * wave, axis=0, keepdims=True)
        far[1, pl.ds(i, 1), :] = jnp.sum(terms[MODES:, lanes] * wave, axis=0, keepdims=True)
    near[...] = (near_a[...] + near_b[...]) + (near_c[...] + near_d[...]) + near_e[...]
    near_last_cols(rows, cols, last, spread, lax.rem(place[1], 2), near)
    live = kept[3] > 0.5
    for part in range(2):
        value = jnp.where(live, near[part] + far[part], 0.0)
        after = kept[part] + section_step * value
        for r in range(rows):
            velocity[part, r] = value[r * cols : (r + 1) * cols]
            moved[part, r] = after[r * cols : (r + 1) * cols]


def far_item(items, index):
    if len(items) == 3:
        return items[2]
    count = 1 << (len(items) - 1)
    up = jnp.where(index % 2 == 1, (index + 1) % count, (index + count - 1) % count)
    mask = index ^ up
    chosen = items[-1]
    for k in range(2, len(items) - 1):
        chosen = jnp.where(mask == (1 << k) - 1, items[k], chosen)
    return chosen


def per_device(offsets, circ, counts):
    rows, cols, slots = circ.shape
    cells = rows * cols
    tx_size, ty_size = lax.axis_size("tx"), lax.axis_size("ty")
    chips = tx_size // 2
    cell_count = rows * tx_size
    tx, ty = lax.axis_index("tx"), lax.axis_index("ty")
    chip = tx // 2
    f32, bf16 = jnp.float32, jnp.bfloat16
    turned = [pltpu.VMEM((slots, 128), f32)]
    near_shape = [((2, cells, slots), f32)]

    first_cell = jnp.stack([ty * cols, tx * rows, tx]).astype(jnp.int32)
    corner = jnp.broadcast_to(first_cell[:, None], (3, slots)).astype(f32)
    own, kept, x_table, y_wave = call(
        functools.partial(moments_kernel, rows, cols, cell_count),
        [
            ((7, cells, slots), f32),
            ((4, cells, slots), f32),
            ((MODES, cells * slots), f32),
            ((MODES, cells * slots), f32),
        ],
        [
            pltpu.VMEM((2, 2, 10 * cells, slots), f32),
            pltpu.VMEM((cells, slots), f32),
        ],
        4_000_000,
        corner, offsets, counts, circ,
    )

    def swap(message, chip_bit, column_bit, flip=True):
        pairs = [
            (i * ty_size + q, ((i // 2 ^ chip_bit) * 2 + (i + flip) % 2) * ty_size + (q ^ column_bit))
            for i in range(tx_size)
            for q in range(ty_size)
        ]
        return lax.ppermute(message, ("tx", "ty"), pairs)

    def near_call(body, flops, *args):
        return call(body, near_shape, turned, flops, *args)[0]

    whole = [(r, c) for c in range(cols) for r in range(rows)]
    third = len(whole) // 4
    partner = swap(own, 0, 0)
    near_a = near_call(
        functools.partial(near_local_kernel, rows, cols, whole[:third]), 4_000_000, own
    )
    tile = (cells, slots)
    six = ((6,) + tile, f32)
    first, across, corner = call(
        functools.partial(join_kernel, rows, cols), [six, ((4,) + tile, f32), six], [], 50_000,
        own, partner,
    )
    message = first
    items = [message]
    bit = 1
    while True:
        if bit == 1:
            sent = (first, across, corner)
        else:
            sent = (message,) * 3
        steps = (1, 2, 3) if 4 * bit <= chips else (1,)
        arrived = [swap(part, step * bit, 0, bit == 1) for step, part in zip(steps, sent)]
        items += arrived[::2]
        bit *= len(steps) + 1
        if bit >= chips:
            break
        message = jnp.concatenate([message[0:4] + sum(got[0:4] for got in arrived), items[-1][4:6]])
    near_b = near_call(
        functools.partial(near_local_kernel, rows, cols, whole[third : 3 * third]), 9_000_000, own
    )
    near_c = near_call(
        functools.partial(near_partner_kernel, rows, cols, whole[3 * third :]), 9_000_000,
        own, partner,
    )
    packed, ring = call(
        functools.partial(pack_kernel, rows, cols),
        [((7,) + tile, f32), ((3,) + tile, f32)], [], 100_000,
        own, partner, message, items[1], far_item(items, chip), *arrived,
    )
    got = swap(packed, 0, 1)
    near_d = near_call(functools.partial(near_ring_kernel, rows, cols), 5_000_000, own, ring)
    message, close = call(
        functools.partial(turn_kernel, rows), [six, ((3, rows + 2, slots), f32)], [], 50_000,
        packed, got,
    )
    items = [None, message]
    bit = 2
    while True:
        got = swap(message, 0, bit, bit == 2)
        items.append(got)
        bit *= 2
        if bit >= ty_size:
            break
        message = jnp.concatenate([message[0:4] + got[0:4], got[4:6]])
    near_e, weights, spread, y_table = call(
        functools.partial(near_close_kernel, rows, cols, cell_count),
        near_shape + [((2, HALF, 2 * MODES), f32), ((2 * rows, slots, slots), f32),
           ((2 * MODES, cells * slots), bf16)],
        turned, 3_000_000,
        own, close, y_wave,
    )
    return tuple(
        call(
            functools.partial(final_kernel, rows, cols),
            [(offsets.shape, f32)] * 2,
            [pltpu.VMEM((2, cells, slots), f32), pltpu.VMEM((2, cells, slots), f32)],
            4_000_000,
            kept, own, x_table, y_table, message, got, far_item(items, ty),
            near_a, near_b, near_c, near_d, near_e, weights, spread,
        )
    )


def solution(mesh):
    placed = (P(None, "tx", "ty", None), P("tx", "ty", None), P("tx", "ty"))

    return jax.shard_map(
        per_device,
        mesh=mesh,
        in_specs=placed,
        out_specs=(P(None, "tx", "ty", None), P(None, "tx", "ty", None)),
        check_vma=False,
    )
```

```python
import functools
import math

import jax
import jax.numpy as jnp
from jax import lax
from jax.experimental import pallas as pl
from jax.experimental.pallas import tpu as pltpu
from jax.sharding import PartitionSpec as P


MODES = 64
HALF = MODES // 2

two_pi = 2.0 * math.pi
screen = 1.5625
smooth = 0.0625
section_step = 0.25
unit = math.sqrt(screen / math.log(2.0))
floor_term = smooth * unit * unit

VMEM = pl.BlockSpec(memory_space=pltpu.VMEM)
PARAMS = pltpu.CompilerParams(vmem_limit_bytes=8 * 1024 * 1024)


def position():
    tx = lax.axis_index("tx")
    return tx, lax.axis_index("ty"), lax.rem(tx, 2)


def call(body, out_shapes, scratch, flops, *args):
    outs = [jax.ShapeDtypeStruct(s, d) for s, d in out_shapes]
    return pl.pallas_call(
        body,
        out_shape=outs,
        in_specs=[VMEM] * len(args),
        out_specs=[VMEM] * len(outs),
        scratch_shapes=scratch,
        compiler_params=PARAMS,
        cost_estimate=pl.CostEstimate(flops=flops, bytes_accessed=65536, transcendentals=0),
    )(*args)


def unit_circle(turn):
    quarter = jnp.floor(4.0 * turn + 0.5)
    angle = two_pi * (turn - 0.25 * quarter)
    sq = angle * angle
    sine = angle * (
        1.0 + sq * (-1.0 / 6 + sq * (1.0 / 120 + sq * (-1.0 / 5040 + sq * (1.0 / 362880))))
    )
    cosine = 1.0 + sq * (
        -0.5 + sq * (1.0 / 24 + sq * (-1.0 / 720 + sq * (1.0 / 40320 + sq * (-1.0 / 3628800))))
    )
    odd = (quarter == 1.0) | (quarter == 3.0)
    cos_neg = (quarter == 1.0) | (quarter == 2.0)
    sin_neg = (quarter == 2.0) | (quarter == 3.0)
    cos_part = jnp.where(odd, sine, cosine)
    sin_part = jnp.where(odd, cosine, sine)
    return jnp.where(cos_neg, -cos_part, cos_part), jnp.where(sin_neg, -sin_part, sin_part)


def times(p, q):
    return p[0] * q[0] - p[1] * q[1], p[0] * q[1] + p[1] * q[0]


def split(value):
    high = value.astype(jnp.bfloat16)
    low = (value - high.astype(jnp.float32)).astype(jnp.bfloat16)
    return high, low


def moments_kernel(
    rows, cols, cell_count, corner_x, corner_y, offsets, counts, circ, own, kept, x_table, y_table,
    powers, amounts,
):
    cells = rows * cols
    slots = circ.shape[2]
    shape = (cells, slots)
    place = position()
    cell = lax.broadcasted_iota(jnp.int32, shape, 0)
    row_in = jnp.zeros(shape, jnp.int32)
    for r in range(1, rows):
        row_in = jnp.where(cell >= r * cols, r, row_in)
    col_in = cell - row_in * cols
    slot = lax.broadcasted_iota(jnp.int32, (1, slots), 1)
    for r in range(rows):
        cells_of = pl.ds(r * cols, cols)
        kept[0, cells_of, :] = offsets[0, r]
        kept[1, cells_of, :] = offsets[1, r]
        for c in range(cols):
            count = jnp.broadcast_to(counts[pl.ds(r, 1), pl.ds(c, 1)], (1, slots))
            kept[3, pl.ds(r * cols + c, 1), :] = jnp.where(slot < count, 1.0, 0.0)
        kept[2, cells_of, :] = jnp.where(kept[3, cells_of, :] > 0.5, circ[r], 0.0)
    off_x, off_y, strength = kept[0], kept[1], kept[2]
    x_turn = ((corner_x[...] + col_in).astype(jnp.float32) + off_x) / cell_count
    y_turn = ((corner_y[...] + row_in).astype(jnp.float32) + off_y) / cell_count
    own[4] = unit * (col_in.astype(jnp.float32) + off_x)
    own[5] = unit * ((place[2] * rows + row_in).astype(jnp.float32) + off_y)
    own[6] = strength * (unit * cell_count / two_pi)
    amounts[...] = strength
    for axis, turn in ((0, x_turn), (1, y_turn)):
        one = unit_circle(turn)
        two = times(one, one)
        three = times(two, one)
        four = times(two, two)
        low_modes = [
            (jnp.ones(shape, jnp.float32), jnp.zeros(shape, jnp.float32)),
            one, two, three, four, times(four, one), times(four, two), times(four, three),
        ]
        eight = times(four, four)
        for k, point in enumerate(low_modes + [eight, times(eight, eight)]):
            for part in range(2):
                powers[axis, part, k * cells : (k + 1) * cells] = point[part]
    full = None
    pair = 2 if cells % 2 == 0 else 1
    for i in range(0, cells, pair):
        left, right = [], []
        for cell_at in range(i, i + pair):
            lanes = pl.ds(cell_at * slots, slots)
            amount = jnp.broadcast_to(amounts[pl.ds(cell_at, 1), :], (8, slots))
            for axis, table, parts in ((0, x_table, left), (1, y_table, right)):

                def row(k, part):
                    at = pl.ds(k * cells + cell_at, 1)
                    return jnp.broadcast_to(powers[axis, part, at, :], (8, slots))

                group = tuple(
                    powers[axis, part, pl.ds(cell_at, 8, stride=cells), :] for part in range(2)
                )
                second = times(group, (row(8, 0), row(8, 1)))
                sixteen = (row(9, 0), row(9, 1))
                groups = [group, second, times(group, sixteen), times(second, sixteen)]
                wave = [g[0] for g in groups] + [g[1] for g in groups]
                table[:, lanes] = jnp.concatenate(wave, axis=0)
                if axis == 0:
                    wave = [piece * amount for piece in wave]
                parts.append(jnp.concatenate(split(jnp.concatenate(wave, axis=0)), axis=0))
        product = lax.dot_general(
            jnp.concatenate(left, axis=1),
            jnp.concatenate(right, axis=1),
            (((1,), (1,)), ((), ())),
            preferred_element_type=jnp.float32,
        )
        full = product if full is None else full + product
    full = full[0:MODES] + full[MODES : 2 * MODES]
    full = full + pltpu.roll(full, MODES, 1)
    lane = lax.broadcasted_iota(jnp.int32, (HALF, 2 * MODES), 1)
    own[0:4] = jnp.where(lane < MODES, full[0:HALF], full[HALF:MODES]).reshape(4, 8, 2 * MODES)


def pair_terms(target, source, total):
    offset_x = target[0] - source[0]
    offset_y = target[1] - source[1]
    square = offset_x * offset_x + offset_y * offset_y
    weight = source[2] / ((square + floor_term) * jnp.exp2(square))
    return total[0] - offset_y * weight, total[1] + offset_x * weight


def near_sum(sources, targets, links, turned, most=48):
    slots = sources[0][0].shape[1]
    stack = [part for source in sources for part in source]
    pad = -len(stack) % 8
    stack = jnp.concatenate(stack + [jnp.zeros((pad, slots), jnp.float32)] * (pad > 0), axis=0)
    turned[:, 0 : stack.shape[0]] = stack.T
    spread = [tuple(jnp.broadcast_to(part, (8, slots)) for part in t) for t in targets]

    def step(k, totals):
        totals = list(totals)
        chunk = turned[pl.ds(8 * k if isinstance(k, int) else pl.multiple_of(8 * k, 8), 8), :]
        for i, reached in enumerate(links):
            source = tuple(
                jnp.broadcast_to(chunk[:, 3 * i + part : 3 * i + part + 1], (8, slots))
                for part in range(3)
            )
            for t in reached:
                totals[2 * t], totals[2 * t + 1] = pair_terms(
                    spread[t], source, (totals[2 * t], totals[2 * t + 1])
                )
        return tuple(totals)

    zero = jnp.zeros((8, slots), jnp.float32)
    pairs = sum(len(reached) for reached in links)
    chunks = slots // 8
    group = 1
    while group * 2 * pairs <= most and chunks % (group * 2) == 0:
        group *= 2

    def grouped(k, totals):
        for u in range(group):
            totals = step(k * group + u, totals)
        return totals

    totals = (zero,) * (2 * len(targets))
    if group == chunks:
        totals = grouped(0, totals)
    else:
        totals = lax.fori_loop(0, chunks // group, grouped, totals)
    return [jnp.sum(total, axis=0, keepdims=True) for total in totals]


def reach(col, cols):
    return [c for c in (col - 1, col, col + 1) if 0 <= c < cols]


def read_row(ref, base, at):
    return tuple(ref[base + part, pl.ds(at, 1), :] for part in range(3))


def near_last_cols(rows, cols, side, spread, right, near):
    slots = side.shape[2]
    shift = jnp.where(right == 1, unit * cols, -unit * cols)
    sources = []
    for k in range(rows + 2):
        row = (
            side[4, pl.ds(k, 1), :] + shift,
            side[4, pl.ds(rows + 2 + k, 1), :],
            side[5, pl.ds(k, 1), :],
        )
        sources.append(tuple(jnp.broadcast_to(part, (8, slots)) for part in row))
    stack = []
    for r in range(rows):
        parts = ([], [])
        for k in range(slots // 8):
            target = tuple(spread[2 * r + part, 8 * k : 8 * k + 8] for part in range(2))
            total = (0.0, 0.0)
            for i in range(r, r + 3):
                total = pair_terms(target, sources[i], total)
            parts[0].append(total[0])
            parts[1].append(total[1])
        stack += parts[0] + parts[1]
    high, low = split(jnp.concatenate(stack, axis=0))
    ones = jnp.ones((8, slots), jnp.bfloat16)

    def lanes_sum(value):
        return lax.dot_general(
            ones, value, (((1,), (1,)), ((), ())), preferred_element_type=jnp.float32
        )

    sums = lanes_sum(high) + lanes_sum(low)
    edge = jnp.where(right == 1, cols - 1, 0)
    for r in range(rows):
        for part in range(2):
            at = pl.ds(r * cols + edge, 1)
            lanes = slice((2 * r + part) * slots, (2 * r + part + 1) * slots)
            near[part, at, :] = near[part, at, :] + sums[0:1, lanes]


def near_local(rows, cols, own, cells, near, turned):
    if not cells:
        return
    places = sorted({(r, c) for row, col in cells for r in range(rows) if abs(r - row) <= 1 for c in reach(col, cols)})
    sources = [read_row(own, 4, r * cols + c) for r, c in cells]
    targets = [read_row(own, 4, r * cols + c)[:2] for r, c in places]
    links = [
        [t for t, (r, c) in enumerate(places) if abs(r - row) <= 1 and abs(c - col) <= 1]
        for row, col in cells
    ]
    sums = near_sum(sources, targets, links, turned)
    for t, (r, c) in enumerate(places):
        for part in range(2):
            at = pl.ds(r * cols + c, 1)
            near[part, at, :] = near[part, at, :] + sums[2 * t + part]


def near_local_kernel(rows, cols, cells, own, near, turned):
    near[...] = jnp.zeros_like(near)
    near_local(rows, cols, own, cells, near, turned)


def near_rows(rows, cols, own, outer, base, above, near, turned):
    def pick(ref, origin, part, first, second):
        return jnp.where(
            above == 1, ref[origin + part, pl.ds(first, 1), :], ref[origin + part, pl.ds(second, 1), :]
        )

    sources = [
        tuple(pick(outer, base, part, cols + c, c) for part in range(3)) for c in range(cols)
    ]
    last = (rows - 1) * cols
    targets = [tuple(pick(own, 4, part, c, last + c) for part in range(2)) for c in range(cols)]
    sums = near_sum(sources, targets, [reach(c, cols) for c in range(cols)], turned)
    top = jnp.where(above == 1, 0, last)
    for c in range(cols):
        for part in range(2):
            at = pl.ds(top + c, 1)
            near[part, at, :] = near[part, at, :] + sums[2 * c + part]


def near_cols(rows, cols, own, side, base, right, near, turned, most=48):
    shift = jnp.where(right == 1, unit * cols, -unit * cols)
    sources = []
    for k in range(rows + 2):
        row = read_row(side, base, k)
        sources.append((row[0] + shift, row[1], row[2]))
    edge = jnp.where(right == 1, cols - 1, 0)
    targets = [read_row(own, 4, r * cols + edge)[:2] for r in range(rows)]
    links = [[r for r in range(rows) if 0 <= k - r <= 2] for k in range(rows + 2)]
    sums = near_sum(sources, targets, links, turned, most)
    for r in range(rows):
        for part in range(2):
            at = pl.ds(r * cols + edge, 1)
            near[part, at, :] = near[part, at, :] + sums[2 * r + part]


def near_partner_kernel(rows, cols, cells, own, partner, near, turned):
    place = position()
    near[...] = jnp.zeros_like(near)
    near_local(rows, cols, own, cells, near, turned)
    near_rows(rows, cols, own, partner, 4, place[2], near, turned)


def near_ring_kernel(rows, cols, own, ring, near, turned):
    place = position()
    near[...] = jnp.zeros_like(near)
    near_rows(rows, cols, own, ring, 0, 1 - place[2], near, turned)


def near_close_kernel(
    rows, cols, cell_count, own, close, y_wave, near, weights, spread, y_table, turned
):
    high, low = split(y_wave[...])
    y_table[0:MODES] = high
    y_table[MODES : 2 * MODES] = low
    shape = (HALF, 2 * MODES)
    lane = lax.broadcasted_iota(jnp.int32, shape, 1)
    m = lax.broadcasted_iota(jnp.int32, shape, 0).astype(jnp.float32)
    n = (lane & (HALF - 1)).astype(jnp.float32)
    square = (two_pi * two_pi) * (m * m + n * n)
    keep = square > 0.0
    safe = jnp.where(keep, square, 1.0)
    damping = jnp.where(keep, jnp.exp(-safe / (6.25 * cell_count * cell_count)) / safe, 0.0)
    damping = damping * (4.0 * two_pi)
    u_weight = damping * n * jnp.where(m == 0.0, 0.5, 1.0)
    v_weight = damping * m * jnp.where(n == 0.0, 0.5, 1.0)
    weights[0] = u_weight
    weights[1] = v_weight
    place = position()
    near[...] = jnp.zeros_like(near)
    right = 1 - lax.rem(place[1], 2)
    slots = own.shape[2]
    edge = jnp.where(right == 1, 0, cols - 1)
    for r in range(rows):
        for part in range(2):
            row = own[4 + part, pl.ds(r * cols + edge, 1), :]
            spread[2 * r + part] = jnp.broadcast_to(row, (slots, slots)).T
    near_cols(rows, cols, own, close, 0, right, near, turned)


def put_row(message, parts):
    message[4] = jnp.concatenate(parts[0:2], axis=0)
    message[5] = jnp.concatenate([parts[2], jnp.zeros_like(parts[2])], axis=0)


def get_row(message, cols):
    return message[4, 0:cols], message[4, cols : 2 * cols], message[5, 0:cols]


def chip_even():
    return lax.rem(lax.div(lax.axis_index("tx"), 2), 2) == 0


def join_kernel(rows, cols, own, partner, message, across, corner):
    core = position()[2]
    last = (rows - 1) * cols
    total = own[0:4] + partner[0:4]
    for target in (message, across, corner):
        target[0:4] = total
    even = chip_even()
    near_parts, far_parts = [], []
    for at in range(4, 7):
        first_row = jnp.where(core == 0, own[at, 0:cols], partner[at, 0:cols])
        last_row = jnp.where(core == 0, partner[at, last:], own[at, last:])
        near_parts.append(jnp.where(even, last_row, first_row))
        far_parts.append(jnp.where(even, first_row, last_row))
    put_row(message, near_parts)
    put_row(corner, far_parts)


def pack_kernel(rows, cols, own, partner, message, near_item, far_item, *others):
    got, (packed, ring) = others[:-2], others[-2:]
    core = position()[2]
    even = chip_even()
    total = message[0:4]
    for item in got:
        total = total + item[0:4]
    packed[0:4] = total
    shift = 2.0 * rows * unit
    for part, (close, distant) in enumerate(zip(get_row(near_item, cols), get_row(far_item, cols))):
        below = jnp.where(even, close, distant)
        above = jnp.where(even, distant, close)
        if part == 1:
            below, above = below + shift, above - shift
        ring[part] = jnp.concatenate([below, above], axis=0)
    near_col = jnp.where(lax.rem(lax.axis_index("ty"), 2) == 0, cols - 1, 0)
    for part in range(3):
        own_of, partner_of = own.at[4 + part], partner.at[4 + part]
        for base, col in ((0, near_col), (rows + 2, cols - 1 - near_col)):

            def cell(ref, r):
                return ref[pl.ds(r * cols + col, 1), :]

            over = ring[part, pl.ds(cols + col, 1), :]
            under = ring[part, pl.ds(col, 1), :]
            mine = [cell(own_of, r) for r in range(rows)]
            other = [cell(partner_of, r) for r in range(rows)]
            if base == 0:
                entries = (
                    [jnp.where(core == 0, mine[-1], over)]
                    + other
                    + [jnp.where(core == 0, under, mine[0])]
                )
            else:
                entries = (
                    [jnp.where(core == 0, over, other[-1])]
                    + mine
                    + [jnp.where(core == 0, other[0], under)]
                )
            for k, entry in enumerate(entries):
                packed[4 + part, pl.ds(base + k, 1), :] = entry


def turn_kernel(rows, packed, got, message, close):
    count = rows + 2
    message[0:4] = packed[0:4] + got[0:4]
    put_row(message, [got[4 + part, count : 2 * count] for part in range(3)])
    for part in range(3):
        close[part, 0:count] = got[4 + part, 0:count]


def final_kernel(
    rows, cols, kept, own, x_table, y_table, message, got, last,
    near_a, near_b, near_c, near_d, near_e, weights, spread, velocity, moved, near, far,
):
    cells = rows * cols
    slots = own.shape[2]
    place = position()
    shape = (HALF, 2 * MODES)
    lane = lax.broadcasted_iota(jnp.int32, shape, 1)
    total = (message[0:4] + got[0:4]).reshape(shape)
    y_odd = (lane & HALF) != 0
    swapped = jnp.where(y_odd, -pltpu.roll(total, HALF, 1), pltpu.roll(total, 2 * MODES - HALF, 1))
    u_part = weights[0] * swapped
    crossed = pltpu.roll(total, MODES, 1)
    v_part = weights[1] * jnp.where(lane < MODES, -crossed, crossed)
    left = []
    for part in (u_part, v_part):
        other = pltpu.roll(part, MODES, 1)
        for doubled in (
            jnp.where(lane < MODES, part, other),
            jnp.where(lane < MODES, other, part),
        ):
            left.append(jnp.concatenate(split(doubled), axis=1))
    left = jnp.concatenate(left, axis=0)
    right = jnp.concatenate([y_table[...], y_table[...]], axis=0)
    terms = jnp.dot(left, right, preferred_element_type=jnp.float32)
    for i in range(cells):
        lanes = slice(i * slots, (i + 1) * slots)
        wave = x_table[:, lanes]
        far[0, pl.ds(i, 1), :] = jnp.sum(terms[0:MODES, lanes] * wave, axis=0, keepdims=True)
        far[1, pl.ds(i, 1), :] = jnp.sum(terms[MODES:, lanes] * wave, axis=0, keepdims=True)
    near[...] = (near_a[...] + near_b[...]) + (near_c[...] + near_d[...]) + near_e[...]
    near_last_cols(rows, cols, last, spread, lax.rem(place[1], 2), near)
    live = kept[3] > 0.5
    for part in range(2):
        value = jnp.where(live, near[part] + far[part], 0.0)
        after = kept[part] + section_step * value
        for r in range(rows):
            velocity[part, r] = value[r * cols : (r + 1) * cols]
            moved[part, r] = after[r * cols : (r + 1) * cols]


def far_item(items, index):
    if len(items) == 3:
        return items[2]
    count = 1 << (len(items) - 1)
    up = jnp.where(index % 2 == 1, (index + 1) % count, (index + count - 1) % count)
    mask = index ^ up
    chosen = items[-1]
    for k in range(2, len(items) - 1):
        chosen = jnp.where(mask == (1 << k) - 1, items[k], chosen)
    return chosen


def per_device(offsets, circ, counts):
    rows, cols, slots = circ.shape
    cells = rows * cols
    tx_size, ty_size = lax.axis_size("tx"), lax.axis_size("ty")
    chips = tx_size // 2
    cell_count = rows * tx_size
    tx, ty = lax.axis_index("tx"), lax.axis_index("ty")
    chip = tx // 2
    f32, bf16 = jnp.float32, jnp.bfloat16
    turned = [pltpu.VMEM((slots, 128), f32)]
    near_shape = [((2, cells, slots), f32)]

    corner_x = jnp.full((1, slots), ty * cols, jnp.int32)
    corner_y = jnp.full((1, slots), tx * rows, jnp.int32)
    own, kept, x_table, y_wave = call(
        functools.partial(moments_kernel, rows, cols, cell_count),
        [
            ((7, cells, slots), f32),
            ((4, cells, slots), f32),
            ((MODES, cells * slots), f32),
            ((MODES, cells * slots), f32),
        ],
        [
            pltpu.VMEM((2, 2, 10 * cells, slots), f32),
            pltpu.VMEM((cells, slots), f32),
        ],
        4_000_000,
        corner_x, corner_y, offsets, counts, circ,
    )

    def swap(message, chip_bit, column_bit, flip=True):
        pairs = [
            (i * ty_size + q, ((i // 2 ^ chip_bit) * 2 + (i + flip) % 2) * ty_size + (q ^ column_bit))
            for i in range(tx_size)
            for q in range(ty_size)
        ]
        return lax.ppermute(message, ("tx", "ty"), pairs)

    def near_call(body, flops, *args):
        return call(body, near_shape, turned, flops, *args)[0]

    whole = [(r, c) for c in range(cols) for r in range(rows)]
    third = len(whole) // 4
    partner = swap(own, 0, 0)
    near_a = near_call(
        functools.partial(near_local_kernel, rows, cols, whole[:third]), 4_000_000, own
    )
    tile = (cells, slots)
    six = ((6,) + tile, f32)
    first, across, corner = call(
        functools.partial(join_kernel, rows, cols), [six, ((4,) + tile, f32), six], [], 50_000,
        own, partner,
    )
    message = first
    items = [message]
    bit = 1
    while True:
        if bit == 1:
            sent = (first, across, corner)
        else:
            sent = (message,) * 3
        steps = (1, 2, 3) if 4 * bit <= chips else (1,)
        arrived = [swap(part, step * bit, 0, bit == 1) for step, part in zip(steps, sent)]
        items += arrived[::2]
        bit *= len(steps) + 1
        if bit >= chips:
            break
        message = jnp.concatenate([message[0:4] + sum(got[0:4] for got in arrived), items[-1][4:6]])
    near_b = near_call(
        functools.partial(near_local_kernel, rows, cols, whole[third : 3 * third]), 9_000_000, own
    )
    near_c = near_call(
        functools.partial(near_partner_kernel, rows, cols, whole[3 * third :]), 9_000_000,
        own, partner,
    )
    packed, ring = call(
        functools.partial(pack_kernel, rows, cols),
        [((7,) + tile, f32), ((3,) + tile, f32)], [], 100_000,
        own, partner, message, items[1], far_item(items, chip), *arrived,
    )
    got = swap(packed, 0, 1)
    near_d = near_call(functools.partial(near_ring_kernel, rows, cols), 5_000_000, own, ring)
    message, close = call(
        functools.partial(turn_kernel, rows), [six, ((3, rows + 2, slots), f32)], [], 50_000,
        packed, got,
    )
    items = [None, message]
    bit = 2
    while True:
        got = swap(message, 0, bit, bit == 2)
        items.append(got)
        bit *= 2
        if bit >= ty_size:
            break
        message = jnp.concatenate([message[0:4] + got[0:4], got[4:6]])
    near_e, weights, spread, y_table = call(
        functools.partial(near_close_kernel, rows, cols, cell_count),
        near_shape + [((2, HALF, 2 * MODES), f32), ((2 * rows, slots, slots), f32),
           ((2 * MODES, cells * slots), bf16)],
        turned, 3_000_000,
        own, close, y_wave,
    )
    return tuple(
        call(
            functools.partial(final_kernel, rows, cols),
            [(offsets.shape, f32)] * 2,
            [pltpu.VMEM((2, cells, slots), f32), pltpu.VMEM((2, cells, slots), f32)],
            4_000_000,
            kept, own, x_table, y_table, message, got, far_item(items, ty),
            near_a, near_b, near_c, near_d, near_e, weights, spread,
        )
    )


def solution(mesh):
    placed = (P(None, "tx", "ty", None), P("tx", "ty", None), P("tx", "ty"))

    return jax.shard_map(
        per_device,
        mesh=mesh,
        in_specs=placed,
        out_specs=(P(None, "tx", "ty", None), P(None, "tx", "ty", None)),
        check_vma=False,
    )
```
